256 devices in a mesh: seq: 64 (over z, x, core), mp: 4 (over y).
Axes of the slice: x: 4, y: 4, z: 8, core: 2. Of those that a mesh axis runs over, the one named last changes fastest.
Arguments:
- branch_in: bfloat16 [32768, 4096], P('seq', 'mp'), may hold values from -48 to 48
- branch_gate: bfloat16 [32768, 4096], P('seq', 'mp'), may hold values from -6 to 6
- conv_taps: float32 [4, 4096], P(None, 'mp'), may hold values from -3 to 3
- conv_shift: float32 [4096], P('mp'), may hold values from -3 to 3
- inflow_weight: bfloat16 [16, 256, 256], P('mp'), may hold values from -0.375 to 0.375
- inflow_bias: float32 [4096], P('mp'), may hold values from -4 to 4
- decay_weight: bfloat16 [16, 256, 256], P('mp'), may hold values from -0.375 to 0.375
- decay_bias: float32 [4096], P('mp'), may hold values from -12 to -1.5
- decay_param: float32 [4096], P('mp'), may hold values from 3 to 4
- stream: bfloat16 [32768, 4096], P('seq', 'mp'), may hold values from -48 to 48
- norm_gain: float32 [4096], P('mp'), may hold values from 0.5 to 1.5
- memory_weight: bfloat16 [4096, 512], P('mp'), may hold values from -1 to 1
- queries: bfloat16 [32768, 4096], P('seq', 'mp'), may hold values from -128 to 128
Outputs:
- recurrent_out: bfloat16 [32768, 4096], P('seq', 'mp')
- attended: bfloat16 [32768, 4096], P('seq', 'mp')
The draws below stay inside these ranges and needn't reach their ends.
All inputs are finite; a program needn't handle non-finite values.
Results may differ from the reference program's by a relative error of at most 0.0071.
Values may be sent and summed in bfloat16 or wider, within the bound.
No kernel may reach another device: no remote copies, remote signals or barrier semaphores. Data moves between devices by JAX's collectives and lax.ppermute only.
A program may use at most 128 MiB of HBM per device.

```python
import jax
import jax.numpy as jnp
from jax import lax

D = 4096
R = 4096
H = 16
HD = 256
RHEADS = 16
CONV = 4
WINDOW = 2048
TOK_DEV = 512
BLK = 256
TOTAL_TOKENS = 32768


def stream_values(key):
    combined_result = jax.random.fold_in(key, 101)
    noise = jax.random.normal(jax.random.fold_in(combined_result, 1), (TOTAL_TOKENS, D), jnp.float32)
    row_scale = jnp.exp(jax.random.uniform(jax.random.fold_in(combined_result, 2), (TOTAL_TOKENS, 1), jnp.float32, jnp.log(0.25), jnp.log(2.5)))
    column_incline = jnp.exp(jnp.linspace(jnp.log(0.6), jnp.log(1.8), D))
    values = noise * column_incline[None, :] * row_scale
    return jnp.clip(values, -48.0, 48.0)


def gain_values(key):
    return jax.random.uniform(jax.random.fold_in(key, 201), (D,), jnp.float32, 0.5, 1.5)


def memory_values(key):
    return jax.random.normal(jax.random.fold_in(key, 301), (D, 2 * HD), jnp.float32) * D ** (-0.5)


def draw_stream(key, part):
    return stream_values(key).astype(jnp.bfloat16)


def draw_norm_gain(key, part):
    return gain_values(key)


def draw_memory_weight(key, part):
    return jnp.clip(memory_values(key), -1.0, 1.0).astype(jnp.bfloat16)


def draw_queries(key, part):
    combined_result = jax.random.fold_in(key, 401)
    values = jax.random.normal(jax.random.fold_in(combined_result, 1), (TOTAL_TOKENS, H * HD), jnp.float32)
    return jnp.clip(values, -128.0, 128.0).astype(jnp.bfloat16)


def draw_branch_in(key, part):
    combined_result = jax.random.fold_in(key, 501)
    values = jax.random.normal(jax.random.fold_in(combined_result, 1), (TOTAL_TOKENS, R), jnp.float32)
    spike_locations = jax.random.randint(jax.random.fold_in(combined_result, 2), (8,), 0, TOTAL_TOKENS)
    raised_values = jnp.zeros((TOTAL_TOKENS,), jnp.float32).at[spike_locations].set(7.0)
    return jnp.clip(values * (1.0 + raised_values)[:, None], -48.0, 48.0).astype(jnp.bfloat16)


def draw_decay_param(key, part):
    rates = jnp.exp(jax.random.uniform(jax.random.fold_in(key, 601), (R,), jnp.float32, jnp.log(0.02), jnp.log(0.04)))
    return -jnp.log(jnp.expm1(rates))


def draw_decay_bias(key, part):
    combined_result = jax.random.fold_in(key, 701)
    quick_share = 0.5
    quick_mask = jax.random.uniform(jax.random.fold_in(combined_result, 1), (R,), jnp.float32) < quick_share
    quick_bias = jax.random.uniform(jax.random.fold_in(combined_result, 2), (R,), jnp.float32, -2.5, -1.8)
    slow_bias = jax.random.uniform(jax.random.fold_in(combined_result, 3), (R,), jnp.float32, -1.3, 0.0) - jnp.log(1.0 * TOK_DEV)
    return jnp.where(quick_mask, quick_bias, slow_bias)


def block_scale(rng, extent, shards, smallest, largest):
    level = 1.0
    for dim, blocks in shards:
        heights = jax.random.uniform(jax.random.fold_in(jax.random.fold_in(rng, 6), dim), (blocks,), jnp.float32, smallest / len(shards), largest / len(shards))
        level = level * jnp.repeat(jnp.exp(heights), extent[dim] // blocks).reshape((-1,) + (1,) * (len(extent) - 1 - dim))
    return level


def centred(rng, extent, spread, reach, split=(), held_as=jnp.bfloat16):
    loudness = block_scale(rng, extent, split, -0.22, 0.18) if split else 1.0
    result = jax.random.normal(rng, extent, jnp.float32) * spread * loudness
    return jnp.minimum(jnp.maximum(result, -reach), reach).astype(held_as)


def setup_inputs(seed: int = 0) -> dict:
    key_list = jax.random.split(jax.random.key(seed), 14)
    branch_in = draw_branch_in(jax.random.fold_in(key_list[13], 71), 0)
    branch_gate = centred(key_list[1], (TOTAL_TOKENS, R), 1.0, 6.0, ((0, 64), (1, 4)))
    conv_taps = centred(key_list[2], (CONV, R), CONV ** -0.5, 3.0, ((1, 4),), jnp.float32)
    conv_shift = centred(key_list[3], (R,), 0.5, 3.0, ((0, 4),), jnp.float32)
    inflow_weight = centred(key_list[4], (RHEADS, BLK, BLK), BLK ** -0.5, 0.375, ((0, 4),))
    inflow_bias = centred(key_list[5], (R,), 1.0, 4.0, ((0, 4),), jnp.float32)
    decay_weight = centred(key_list[6], (RHEADS, BLK, BLK), BLK ** -0.5, 0.375, ((0, 4),))
    decay_bias = draw_decay_bias(jax.random.fold_in(key_list[13], 71), 0)
    decay_param = draw_decay_param(jax.random.fold_in(key_list[13], 71), 0)
    stream = draw_stream(jax.random.fold_in(key_list[13], 71), 0)
    norm_gain = draw_norm_gain(jax.random.fold_in(key_list[13], 71), 0)
    memory_weight = draw_memory_weight(jax.random.fold_in(key_list[13], 71), 0)
    queries = draw_queries(jax.random.fold_in(key_list[13], 71), 0)
    return dict(branch_in=branch_in, branch_gate=branch_gate, conv_taps=conv_taps, conv_shift=conv_shift, inflow_weight=inflow_weight, inflow_bias=inflow_bias, decay_weight=decay_weight, decay_bias=decay_bias, decay_param=decay_param, stream=stream, norm_gain=norm_gain, memory_weight=memory_weight, queries=queries)


decay_power = 8.0
norm_epsilon = 1e-06
masked_score = -1e+30

def convolve(branch_in, conv_taps, conv_shift):
    inputs = branch_in.astype(jnp.float32)
    totals = conv_shift[None, :] + conv_taps[0][None, :] * inputs
    for offset in range(1, CONV):
        delayed = jnp.concatenate([jnp.zeros((offset, inputs.shape[1]), jnp.float32), inputs[:-offset]], axis=0)
        totals = totals + conv_taps[offset][None, :] * delayed
    return totals.astype(jnp.bfloat16)

def attend_block(query_block, window_block, query_start, key_start, head_count):
    token_rows = query_block.shape[0]
    key_count = window_block.shape[0]
    grouped = query_block.astype(jnp.float32).reshape(token_rows, head_count, HD)
    key_rows = window_block[:, :HD].astype(jnp.float32)
    value_rows = window_block[:, HD:].astype(jnp.float32)
    scores = jnp.einsum('qhd,kd->hqk', grouped, key_rows, precision=lax.Precision.HIGHEST) * HD ** (-0.5)
    query_pos = query_start + jnp.arange(token_rows, dtype=jnp.int32)
    key_pos = key_start + jnp.arange(key_count, dtype=jnp.int32)
    distance = query_pos[:, None] - key_pos[None, :]
    allowed = (distance >= 0) & (distance < WINDOW) & (key_pos[None, :] >= 0)
    scores = jnp.where(allowed[None], scores, masked_score)
    row_peak = lax.optimization_barrier(jnp.max(scores, axis=2, keepdims=True))
    weights = jnp.exp(scores - row_peak)
    softmax_probs = (weights / lax.optimization_barrier(jnp.sum(weights, axis=2, keepdims=True))).astype(jnp.bfloat16)
    output = jnp.einsum('hqk,kd->qhd', softmax_probs.astype(jnp.float32), value_rows, precision=lax.Precision.HIGHEST)
    return output.reshape(token_rows, head_count * HD).astype(jnp.bfloat16)

def reference(branch_in, branch_gate, conv_taps, conv_shift, inflow_weight, inflow_bias, decay_weight, decay_bias, decay_param, stream, norm_gain, memory_weight, queries):
    mixed_conv = convolve(branch_in, conv_taps, conv_shift)
    block_count = TOTAL_TOKENS // TOK_DEV
    inflow_full = inflow_weight.astype(jnp.float32)
    decay_full = decay_weight.astype(jnp.float32)
    softened = jax.nn.softplus(-decay_param)

    def run_block(carried, block_pair):
        conv_block, gate_block = block_pair
        conv_float = conv_block.astype(jnp.float32)
        grouped = conv_float.reshape(TOK_DEV, RHEADS, BLK)
        inflow = jax.nn.sigmoid(jnp.einsum('tnb,nbc->tnc', grouped, inflow_full, precision=lax.Precision.HIGHEST).reshape(TOK_DEV, R) + inflow_bias[None, :])
        recurrence = jax.nn.sigmoid(jnp.einsum('tnb,nbc->tnc', grouped, decay_full, precision=lax.Precision.HIGHEST).reshape(TOK_DEV, R) + decay_bias[None, :])
        log_decay = -decay_power * recurrence * softened[None, :]
        factor = jnp.exp(log_decay)
        pushed = jnp.sqrt(-jnp.expm1(2.0 * log_decay)) * inflow * conv_float

        def tick(current, entries):
            updated = entries[0] * current + entries[1]
            return (updated, updated)
        carried, history = lax.scan(tick, carried, (factor, pushed))
        output = (history * jax.nn.gelu(gate_block.astype(jnp.float32), approximate=True)).astype(jnp.bfloat16)
        return (carried, output)
    _, outputs = lax.scan(run_block, jnp.zeros((R,), jnp.float32), (mixed_conv.reshape(block_count, TOK_DEV, R), branch_gate.reshape(block_count, TOK_DEV, R)))
    recurrent_out = outputs.reshape(TOTAL_TOKENS, R)
    stream_float = stream.astype(jnp.float32)
    squares = lax.optimization_barrier(jnp.sum(jnp.square(stream_float), axis=1))
    scaled = (stream_float * norm_gain[None, :]).astype(jnp.bfloat16)
    raw_memory = jnp.dot(scaled, memory_weight, preferred_element_type=jnp.float32)
    memory = (raw_memory / jnp.sqrt(squares / D + norm_epsilon)[:, None]).astype(jnp.bfloat16)
    padded = jnp.concatenate([jnp.zeros((WINDOW, 2 * HD), jnp.bfloat16), memory], axis=0)

    def attend(block_index):
        block_start = (block_index * TOK_DEV).astype(jnp.int32)
        query_block = lax.dynamic_slice_in_dim(queries, block_start, TOK_DEV, 0)
        window_block = lax.dynamic_slice_in_dim(padded, block_start, WINDOW + TOK_DEV, 0)
        return attend_block(query_block, window_block, block_start, block_start - WINDOW, H)
    attended = lax.map(attend, jnp.arange(block_count, dtype=jnp.int32)).reshape(TOTAL_TOKENS, H * HD)
    return (recurrent_out, attended)
```

```python
import functools

import jax
import jax.numpy as jnp
from jax import lax
from jax.experimental import pallas as pl
from jax.experimental.pallas import tpu as pltpu
from jax.sharding import Mesh
from jax.sharding import PartitionSpec as P

D = 4096
HD = 256
CONV = 4
WINDOW = 2048
BLK = 256
SEQ = ("seq_0", "seq_1", "seq_2")
CORE = "seq_2"
TOK = 512
QUARTER = 128
PARTS = 4
SEGMENTS = 8
STEPS = TOK // SEGMENTS
QROWS = 256
LANES = 128

decay_power = 8.0
norm_epsilon = 1e-06
masked_score = -1e30
F32 = jnp.float32
BF16 = jnp.bfloat16
SMEM = pl.BlockSpec(memory_space=pltpu.SMEM)


def whole(shape):
    return pl.BlockSpec(shape, lambda *_: (0,) * len(shape))


def shifted(value, steps):
    count = lax.axis_size(SEQ)
    return lax.ppermute(value, SEQ, [(k, k + steps) for k in range(count - steps)])


def turned(value, steps):
    return lax.ppermute(value, "mp", [(k, (k + steps) % PARTS) for k in range(PARTS)])


def swapped(value):
    return lax.ppermute(value, CORE, [(0, 1), (1, 0)])


def project_kernel(place, stream, gain, weight, *parts):
    for k, part in enumerate(parts):
        start = pl.multiple_of(lax.rem(place[0] + k, PARTS) * QUARTER, QUARTER)
        x = stream[pl.ds(start, QUARTER), :].astype(F32)
        squares = jnp.sum(x * x, axis=1, keepdims=True)
        scaled = (x * gain[...]).astype(BF16)
        part[0:QUARTER, :] = jnp.dot(scaled, weight[...], preferred_element_type=F32)
        part[QUARTER:, :] = jnp.zeros((8, 2 * HD), F32)
        part[QUARTER:, 0:QUARTER] = jnp.broadcast_to(squares, (QUARTER, QUARTER)).T[0:8]


def project(place, stream, gain, weight):
    shape = (QUARTER + 8, 2 * HD)
    return pl.pallas_call(
        project_kernel,
        name="project",
        out_shape=[jax.ShapeDtypeStruct(shape, F32)] * PARTS,
        in_specs=[SMEM, whole(stream.shape), whole(gain.shape), whole(weight.shape)],
        out_specs=[whole(shape)] * PARTS,
        compiler_params=pltpu.CompilerParams(vmem_limit_bytes=24 << 20),
        cost_estimate=pl.CostEstimate(flops=1 << 29, bytes_accessed=3 << 20, transcendentals=0),
    )(place, stream, gain, weight)


def norm_kernel(a, b, c, d, out):
    total = (a[...] + b[...]) + (c[...] + d[...])
    row = jnp.broadcast_to(total[QUARTER : QUARTER + 1, 0:QUARTER], (QUARTER, QUARTER))
    column = row.T[:, 0:1]
    root = jnp.sqrt(column / D + norm_epsilon)
    out[...] = (total[0:QUARTER] / root).astype(BF16)


def normed(parts):
    shape = (QUARTER, 2 * HD)
    return pl.pallas_call(
        norm_kernel,
        name="normed",
        out_shape=jax.ShapeDtypeStruct(shape, BF16),
        in_specs=[whole(parts[0].shape)] * PARTS,
        out_specs=whole(shape),
        cost_estimate=pl.CostEstimate(flops=1 << 20, bytes_accessed=5 << 18, transcendentals=0),
    )(*parts)


def join_kernel(place, *refs):
    out = refs[PARTS]
    for k in range(PARTS):
        start = pl.multiple_of(lax.rem(place[0] + PARTS - k, PARTS) * QUARTER, QUARTER)
        out[pl.ds(start, QUARTER), :] = refs[k][...]


def joined(place, pieces):
    shape = (TOK, 2 * HD)
    return pl.pallas_call(
        join_kernel,
        name="joined",
        out_shape=jax.ShapeDtypeStruct(shape, BF16),
        in_specs=[SMEM] + [whole(pieces[0].shape)] * PARTS,
        out_specs=whole(shape),
        cost_estimate=pl.CostEstimate(flops=0, bytes_accessed=1 << 20, transcendentals=0),
    )(place, *pieces)


def negative_expm1(y, grown):
    series = jnp.full_like(y, 1.0)
    for k in (8, 7, 6, 5, 4, 3, 2):
        series = 1.0 + series * (y * (1.0 / k))
    return jnp.where(y > -0.5, -y * series, 1.0 - grown)


def recur_kernel(
    branch, edge, gate, taps, shift, in_w, in_b, de_w, de_b, param, u_out, w_out, end_out,
    extended, factors, pushes,
):
    extended[8 : 8 + TOK, :] = branch[...].astype(F32)
    extended[8 - (CONV - 1) : 8, :] = edge[...].astype(F32)
    totals = shift[...] + taps[0:1, :] * extended[8 : 8 + TOK, :]
    for k in range(1, CONV):
        totals = totals + taps[k : k + 1, :] * extended[8 - k : 8 - k + TOK, :]
    mixed = totals.astype(BF16)
    inflow = jax.nn.sigmoid(
        jnp.dot(mixed, in_w[0], preferred_element_type=F32) + in_b[...]
    )
    recurrence = jax.nn.sigmoid(
        jnp.dot(mixed, de_w[0], preferred_element_type=F32) + de_b[...]
    )
    v = -param[...]
    soft = jnp.maximum(v, 0.0) + jnp.log1p(jnp.exp(-jnp.abs(v)))
    log_decay = recurrence * (-decay_power * soft)
    factor = jnp.exp(log_decay)
    push = (
        jnp.sqrt(negative_expm1(2.0 * log_decay, factor * factor))
        * inflow
        * mixed.astype(F32)
    )
    for lane in range(BLK // LANES):
        there = slice(lane * LANES, (lane + 1) * LANES)
        factors[lane] = factor[:, there]
        pushes[lane] = push[:, there]

    lanes = range(BLK // LANES)
    product = [jnp.ones((SEGMENTS, LANES), F32) for _ in lanes]
    state = [jnp.zeros((SEGMENTS, LANES), F32) for _ in lanes]
    for t in range(STEPS):
        rows = pl.ds(t, SEGMENTS, stride=STEPS)
        for lane in lanes:
            f = factors[lane, rows, :]
            state[lane] = f * state[lane] + pushes[lane, rows, :]
            product[lane] = product[lane] * f
            pushes[lane, rows, :] = state[lane]
            factors[lane, rows, :] = product[lane]
    for lane in lanes:
        there = slice(lane * LANES, (lane + 1) * LANES)
        before_f = jnp.ones((1, LANES), F32)
        before_s = jnp.zeros((1, LANES), F32)
        for r in range(SEGMENTS):
            rows = slice(r * STEPS, (r + 1) * STEPS)
            g = gate[rows, there].astype(F32)
            g = 0.5 * g * (1.0 + jnp.tanh(0.7978845608028654 * (g + 0.044715 * (g * g * g))))
            local_f = factors[lane, rows, :]
            u_out[rows, there] = (pushes[lane, rows, :] + local_f * before_s) * g
            w_out[rows, there] = (local_f * before_f) * g
            before_s = product[lane][r : r + 1] * before_s + state[lane][r : r + 1]
            before_f = product[lane][r : r + 1] * before_f
        end_out[0:1, there] = before_f
        end_out[1:2, there] = before_s


def recur(branch, edge, gate, taps, shift, in_w, in_b, de_w, de_b, param):
    channels = branch.shape[1]
    groups = channels // BLK
    lane = lambda rows: pl.BlockSpec((rows, BLK), lambda n: (0, n))
    square = pl.BlockSpec((1, BLK, BLK), lambda n: (n, 0, 0))
    return pl.pallas_call(
        recur_kernel,
        name="recur",
        grid=(groups,),
        out_shape=[
            jax.ShapeDtypeStruct((TOK, channels), F32),
            jax.ShapeDtypeStruct((TOK, channels), F32),
            jax.ShapeDtypeStruct((2, channels), F32),
        ],
        in_specs=[
            lane(TOK), lane(CONV - 1), lane(TOK), lane(CONV), lane(1),
            square, lane(1), square, lane(1), lane(1),
        ],
        out_specs=[lane(TOK), lane(TOK), lane(2)],
        scratch_shapes=[
            pltpu.VMEM((TOK + 8, BLK), F32),
            pltpu.VMEM((BLK // LANES, TOK, LANES), F32),
            pltpu.VMEM((BLK // LANES, TOK, LANES), F32),
        ],
        compiler_params=pltpu.CompilerParams(vmem_limit_bytes=24 << 20),
        cost_estimate=pl.CostEstimate(
            flops=1 << 30, bytes_accessed=8 << 20, transcendentals=1 << 22
        ),
    )(branch, edge, gate, taps, shift, in_w, in_b, de_w, de_b, param)


def attend_kernel(
    info, q_ref, own, back2, back4, swap0, swap1, swap2, u, w, state, out, recurrent_out, chosen
):
    core, position = (info[0], info[1])
    recurrent_out[...] = (u[...] + w[...] * state[...]).astype(BF16)

    @pl.when(pl.program_id(0) == 0)
    def _():
        @pl.when(core == 0)
        def _():
            chosen[...] = swap2[...]

        @pl.when(core != 0)
        def _():
            chosen[...] = swap0[...]

    def bias(behind):
        return jnp.where(position >= behind, 0.0, masked_score).astype(F32)

    first = bias(1 + 2 * core)
    second = bias(3 - 2 * core)
    rows = lax.broadcasted_iota(jnp.int32, (QROWS, QROWS), 0)
    columns = lax.broadcasted_iota(jnp.int32, (QROWS, QROWS), 1)
    causal = rows >= columns
    halves = (slice(0, QROWS), slice(QROWS, TOK))
    full = slice(0, TOK)
    for half in range(2):
        q = q_ref[halves[half], :] * jnp.asarray(HD**-0.5, BF16)
        blocks = [
            (back2, full, bias(2), None),
            (swap1, full, first, None),
            (chosen, full, second, None),
            (back4, halves[half], bias(4), ~causal),
        ]
        if half == 0:
            blocks.append((back4, halves[1], bias(4), None))
        else:
            blocks.append((own, halves[0], None, None))
        blocks.append((own, halves[half], None, causal))
        scores = []
        for ref, keys, extra, mask in blocks:
            s = lax.dot_general(
                q, ref[keys, 0:HD], (((1,), (1,)), ((), ())), preferred_element_type=F32
            )
            if extra is not None:
                s = s + extra
            if mask is not None:
                s = jnp.where(mask, s, masked_score)
            scores.append(s)
        tiles = [s[:, k : k + 128] for s in scores for k in range(0, s.shape[1], 128)]
        peak = jnp.max(functools.reduce(jnp.maximum, tiles), axis=1, keepdims=True)
        weights = [jnp.exp(s - peak) for s in scores]
        tiles = [p[:, k : k + 128] for p in weights for k in range(0, p.shape[1], 128)]
        norm = jnp.sum(functools.reduce(jnp.add, tiles), axis=1, keepdims=True)
        total = jnp.zeros((QROWS, HD), F32)
        for p, (ref, keys, _, _) in zip(weights, blocks):
            total = total + jnp.dot(
                p.astype(BF16), ref[keys, HD:], preferred_element_type=F32
            )
        out[halves[half], :] = (total / norm).astype(BF16)


def attend(info, queries, shards_of_memory, u, w, state):
    heads = queries.shape[1] // HD
    head = pl.BlockSpec((TOK, HD), lambda h: (0, h))
    one = pl.BlockSpec((1, HD), lambda h: (0, h))
    memory = whole((TOK, 2 * HD))
    return pl.pallas_call(
        attend_kernel,
        name="attend",
        grid=(heads,),
        out_shape=[jax.ShapeDtypeStruct(queries.shape, BF16)] * 2,
        in_specs=[SMEM, head] + [memory] * 6 + [head, head, one],
        out_specs=[head, head],
        scratch_shapes=[pltpu.VMEM((TOK, 2 * HD), BF16)],
        compiler_params=pltpu.CompilerParams(vmem_limit_bytes=40 << 20),
        cost_estimate=pl.CostEstimate(
            flops=5 << 30, bytes_accessed=10 << 20, transcendentals=5 << 20
        ),
    )(info, queries, *shards_of_memory, u, w, state)


def compose(earlier, later):
    return jnp.stack([earlier[0] * later[0], later[0] * earlier[1] + later[1]])


def entering(couple, core):
    other = swapped(couple)
    first = core == 0
    inclusive = compose(jnp.where(first, couple, other), jnp.where(first, other, couple))
    empty = jnp.stack([jnp.ones_like(couple[0]), jnp.zeros_like(couple[0])])
    before = jnp.where(first, empty, other)
    steps = 2
    while steps < lax.axis_size(SEQ):
        arrived = shifted(inclusive, steps)
        before = compose(arrived, before)
        inclusive = compose(arrived, inclusive)
        steps *= 2
    return before[1:2]


def shards(
    branch_in,
    branch_gate,
    conv_taps,
    conv_shift,
    inflow_weight,
    inflow_bias,
    decay_weight,
    decay_bias,
    decay_param,
    stream,
    norm_gain,
    memory_weight,
    queries,
):
    position = lax.axis_index(SEQ)
    core = lax.axis_index(CORE)
    place = lax.axis_index("mp").reshape(1)
    info = jnp.stack([core, position]).astype(jnp.int32)
    line = lambda v: v.reshape(1, -1)

    edge = shifted(branch_in[TOK - (CONV - 1) :], 1)
    parts = project(place, stream, line(norm_gain), memory_weight)
    edge, *parts = lax.optimization_barrier((edge, *parts))
    arrived = [turned(parts[k], k) for k in range(1, PARTS)]
    u, w, couple = recur(
        branch_in, edge, branch_gate, conv_taps, line(conv_shift),
        inflow_weight, line(inflow_bias), decay_weight, line(decay_bias), line(decay_param),
    )
    quarter = normed([parts[0]] + arrived)
    quarter, couple = lax.optimization_barrier((quarter, couple))
    pieces = [quarter] + [turned(quarter, k) for k in range(1, PARTS)]
    memory = joined(place, pieces)
    back2 = shifted(memory, 2)
    back4 = shifted(memory, 4)
    swap0, swap1, swap2 = (swapped(memory), swapped(back2), swapped(back4))
    incoming = entering(couple, core)
    window = (memory, back2, back4, swap0, swap1, swap2)
    attended, recurrent_out = attend(info, queries, window, u, w, incoming)
    return (recurrent_out, attended)


def solution(mesh):
    finer = Mesh(mesh.devices.reshape(8, 4, 2, mesh.shape["mp"]), (*SEQ, "mp"))
    in_specs = (
        P(SEQ, "mp"),
        P(SEQ, "mp"),
        P(None, "mp"),
        P("mp"),
        P("mp", None, None),
        P("mp"),
        P("mp", None, None),
        P("mp"),
        P("mp"),
        P(SEQ, "mp"),
        P("mp"),
        P("mp", None),
        P(SEQ, "mp"),
    )
    out_specs = (P(SEQ, "mp"), P(SEQ, "mp"))
    return jax.shard_map(
        shards, mesh=finer, in_specs=in_specs, out_specs=out_specs, check_vma=False
    )
```

```python
import functools

import jax
import jax.numpy as jnp
from jax import lax
from jax.experimental import pallas as pl
from jax.experimental.pallas import tpu as pltpu
from jax.sharding import Mesh
from jax.sharding import PartitionSpec as P

D = 4096
HD = 256
CONV = 4
WINDOW = 2048
BLK = 256
SEQ = ("seq_0", "seq_1", "seq_2")
CORE = "seq_2"
TOK = 512
QUARTER = 128
PARTS = 4
SEGMENTS = 8
STEPS = TOK // SEGMENTS
QROWS = 256
LANES = 128
EXTRA = 16
ROOM = 60 << 20
SHARDS = 5

decay_power = 8.0
norm_epsilon = 1e-06
masked_score = -1e30
F32 = jnp.float32
BF16 = jnp.bfloat16
SMEM = pl.BlockSpec(memory_space=pltpu.SMEM)


def whole(shape):
    return pl.BlockSpec(shape, lambda *_: (0,) * len(shape))


def shifted(value, steps):
    count = lax.axis_size(SEQ)
    return lax.ppermute(value, SEQ, [(k, k + steps) for k in range(count - steps)])


def turned(value, steps):
    return lax.ppermute(value, "mp", [(k, (k + steps) % PARTS) for k in range(PARTS)])


def swapped(value):
    return lax.ppermute(value, CORE, [(0, 1), (1, 0)])


def project_kernel(place, stream, gain, weight, *parts):
    row = lax.broadcasted_iota(jnp.int32, (EXTRA, QUARTER), 0)
    for k, part in enumerate(parts):
        start = pl.multiple_of(lax.rem(place[0] + k, PARTS) * QUARTER, QUARTER)
        x = stream[pl.ds(start, QUARTER), :].astype(F32)
        squares = jnp.sum(x * x, axis=1, keepdims=True)
        scaled = (x * gain[...]).astype(BF16)
        product = jnp.dot(scaled, weight[...], preferred_element_type=F32)
        part[0:QUARTER, :] = product.astype(part.dtype)
        part[QUARTER:, :] = jnp.zeros((EXTRA, 2 * HD), part.dtype)
        line = jnp.broadcast_to(squares, (QUARTER, QUARTER)).T[0:EXTRA]
        high = line.astype(BF16).astype(F32)
        line = jnp.where(row == 0, high, jnp.where(row == 1, line - high, 0.0))
        part[QUARTER:, 0:QUARTER] = line.astype(part.dtype)


def project(place, stream, gain, weight):
    shape = (QUARTER + EXTRA, 2 * HD)
    return pl.pallas_call(
        project_kernel,
        name="project",
        out_shape=[jax.ShapeDtypeStruct(shape, F32 if k == 0 else BF16) for k in range(PARTS)],
        in_specs=[SMEM, whole(stream.shape), whole(gain.shape), whole(weight.shape)],
        out_specs=[whole(shape)] * PARTS,
        compiler_params=pltpu.CompilerParams(vmem_limit_bytes=ROOM),
        cost_estimate=pl.CostEstimate(flops=1 << 29, bytes_accessed=3 << 20, transcendentals=0),
    )(place, stream, gain, weight)


def norm_kernel(a, b, c, d, out):
    total = (a[...] + b[...].astype(F32)) + (c[...].astype(F32) + d[...].astype(F32))
    line = total[QUARTER : QUARTER + 1, 0:QUARTER] + total[QUARTER + 1 : QUARTER + 2, 0:QUARTER]
    column = jnp.broadcast_to(line, (QUARTER, QUARTER)).T[:, 0:1]
    root = jnp.sqrt(column / D + norm_epsilon)
    out[...] = (total[0:QUARTER] / root).astype(BF16)


def normed(parts):
    shape = (QUARTER, 2 * HD)
    return pl.pallas_call(
        norm_kernel,
        name="normed",
        out_shape=jax.ShapeDtypeStruct(shape, BF16),
        in_specs=[whole(parts[0].shape)] * PARTS,
        out_specs=whole(shape),
        compiler_params=pltpu.CompilerParams(vmem_limit_bytes=8 << 20),
        cost_estimate=pl.CostEstimate(flops=1 << 20, bytes_accessed=5 << 17, transcendentals=0),
    )(*parts)


def negative_expm1(y, grown):
    series = jnp.full_like(y, 1.0)
    for k in (8, 7, 6, 5, 4, 3, 2):
        series = 1.0 + series * (y * (1.0 / k))
    return jnp.where(y > -0.5, -y * series, 1.0 - grown)


def recur_kernel(
    branch, edge, gate, taps, shift, in_w, in_b, de_w, de_b, param, *rest
):
    u_out, w_out, end_out, extended, factors, pushes = rest[-6:]
    extended[8 : 8 + TOK, :] = branch[...].astype(F32)
    extended[8 - (CONV - 1) : 8, :] = edge[...].astype(F32)
    totals = shift[...] + taps[0:1, :] * extended[8 : 8 + TOK, :]
    for k in range(1, CONV):
        totals = totals + taps[k : k + 1, :] * extended[8 - k : 8 - k + TOK, :]
    mixed = totals.astype(BF16)
    inflow = jax.nn.sigmoid(
        jnp.dot(mixed, in_w[0], preferred_element_type=F32) + in_b[...]
    )
    recurrence = jax.nn.sigmoid(
        jnp.dot(mixed, de_w[0], preferred_element_type=F32) + de_b[...]
    )
    v = -param[...]
    soft = jnp.maximum(v, 0.0) + jnp.log1p(jnp.exp(-jnp.abs(v)))
    log_decay = recurrence * (-decay_power * soft)
    factor = jnp.exp(log_decay)
    push = (
        jnp.sqrt(negative_expm1(2.0 * log_decay, factor * factor))
        * inflow
        * mixed.astype(F32)
    )
    for lane in range(BLK // LANES):
        there = slice(lane * LANES, (lane + 1) * LANES)
        factors[lane] = factor[:, there]
        pushes[lane] = push[:, there]

    lanes = range(BLK // LANES)
    product = [jnp.ones((SEGMENTS, LANES), F32) for _ in lanes]
    state = [jnp.zeros((SEGMENTS, LANES), F32) for _ in lanes]
    for t in range(STEPS):
        rows = pl.ds(t, SEGMENTS, stride=STEPS)
        for lane in lanes:
            f = factors[lane, rows, :]
            state[lane] = f * state[lane] + pushes[lane, rows, :]
            product[lane] = product[lane] * f
            pushes[lane, rows, :] = state[lane]
            factors[lane, rows, :] = product[lane]
    for lane in lanes:
        there = slice(lane * LANES, (lane + 1) * LANES)
        before_f = jnp.ones((1, LANES), F32)
        before_s = jnp.zeros((1, LANES), F32)
        for r in range(SEGMENTS):
            rows = slice(r * STEPS, (r + 1) * STEPS)
            g = gate[rows, there].astype(F32)
            g = 0.5 * g * (1.0 + jnp.tanh(0.7978845608028654 * (g + 0.044715 * (g * g * g))))
            local_f = factors[lane, rows, :]
            u_out[rows, there] = (pushes[lane, rows, :] + local_f * before_s) * g
            w_out[rows, there] = (local_f * before_f) * g
            before_s = product[lane][r : r + 1] * before_s + state[lane][r : r + 1]
            before_f = product[lane][r : r + 1] * before_f
        end_out[0:1, there] = before_f
        end_out[1:2, there] = before_s


def recur(group, count, branch, edge, gate, taps, shift, in_w, in_b, de_w, de_b, param, filled):
    channels = branch.shape[1]
    lane = lambda rows: pl.BlockSpec((rows, BLK), lambda n: (0, n + group))
    square = pl.BlockSpec((1, BLK, BLK), lambda n: (n + group, 0, 0))
    kept = pl.BlockSpec(memory_space=pl.ANY)
    inputs = (branch, edge, gate, taps, shift, in_w, in_b, de_w, de_b, param)
    return pl.pallas_call(
        recur_kernel,
        name="recur",
        grid=(count,),
        out_shape=[
            jax.ShapeDtypeStruct((TOK, channels), F32),
            jax.ShapeDtypeStruct((TOK, channels), F32),
            jax.ShapeDtypeStruct((2, channels), F32),
        ],
        in_specs=[
            lane(TOK), lane(CONV - 1), lane(TOK), lane(CONV), lane(1),
            square, lane(1), square, lane(1), lane(1),
        ] + [kept] * len(filled),
        out_specs=[lane(TOK), lane(TOK), lane(2)],
        scratch_shapes=[
            pltpu.VMEM((TOK + 8, BLK), F32),
            pltpu.VMEM((BLK // LANES, TOK, LANES), F32),
            pltpu.VMEM((BLK // LANES, TOK, LANES), F32),
        ],
        input_output_aliases={len(inputs) + k: k for k in range(len(filled))},
        compiler_params=pltpu.CompilerParams(vmem_limit_bytes=ROOM),
        cost_estimate=pl.CostEstimate(
            flops=count << 28, bytes_accessed=count << 21, transcendentals=count << 20
        ),
    )(*inputs, *filled)


def attend_kernel(info, q_ref, *refs):
    own, other = (refs[0:PARTS], refs[PARTS : 2 * PARTS])
    out, kv = refs[-2:]
    core, position, place = (info[0], info[1], info[2])

    @pl.when(pl.program_id(0) == 0)
    def _():
        for k in range(PARTS):
            row = lax.rem(place + PARTS - k, PARTS) * QUARTER
            for behind in range(SHARDS):
                there = pl.ds(
                    pl.multiple_of((SHARDS - 1 - behind) * TOK + row, QUARTER), QUARTER
                )
                if behind % 2 == 0:
                    kv[there, :] = own[k][behind // 2 * QUARTER : (behind // 2 + 1) * QUARTER, :]
                else:
                    begin = pl.multiple_of(((behind + 1) // 2 - core) * QUARTER, QUARTER)
                    kv[there, :] = other[k][pl.ds(begin, QUARTER), :]

    def bias(behind):
        return jnp.where(position >= behind, 0.0, masked_score).astype(F32)

    rows = lax.broadcasted_iota(jnp.int32, (QROWS, QROWS), 0)
    columns = lax.broadcasted_iota(jnp.int32, (QROWS, QROWS), 1)
    causal = rows >= columns
    last = (SHARDS - 1) * TOK
    for half in range(2):
        low = half * QROWS
        q = q_ref[low : low + QROWS, :] * jnp.asarray(HD**-0.5, BF16)
        blocks = [(k * TOK, TOK, bias(SHARDS - 1 - k), None) for k in range(1, SHARDS - 1)]
        if half == 0:
            blocks.append((QROWS, QROWS, bias(SHARDS - 1), None))
        else:
            blocks.append((last, QROWS, None, None))
        blocks.append((low, QROWS, bias(SHARDS - 1), ~causal))
        blocks.append((last + low, QROWS, None, causal))
        scores = []
        for begin, size, extra, mask in blocks:
            s = lax.dot_general(
                q,
                kv[begin : begin + size, 0:HD],
                (((1,), (1,)), ((), ())),
                preferred_element_type=F32,
            )
            if extra is not None:
                s = s + extra
            if mask is not None:
                s = jnp.where(mask, s, masked_score)
            scores.append(s)
        tiles = [s[:, k : k + 128] for s in scores for k in range(0, s.shape[1], 128)]
        peak = jnp.max(functools.reduce(jnp.maximum, tiles), axis=1, keepdims=True)
        weights = [jnp.exp(s - peak) for s in scores]
        tiles = [p[:, k : k + 128] for p in weights for k in range(0, p.shape[1], 128)]
        norm = jnp.sum(functools.reduce(jnp.add, tiles), axis=1, keepdims=True)
        total = jnp.zeros((QROWS, HD), F32)
        for p, (begin, size, _, _) in zip(weights, blocks):
            total = total + jnp.dot(
                p.astype(BF16), kv[begin : begin + size, HD:], preferred_element_type=F32
            )
        out[low : low + QROWS, :] = (total / norm).astype(BF16)


def attend(head, count, info, queries, own, other, filled):
    block = pl.BlockSpec((TOK, HD), lambda h: (0, h + head))
    kept = pl.BlockSpec(memory_space=pl.ANY)
    inputs = (info, queries, *own, *other)
    return pl.pallas_call(
        attend_kernel,
        name="attend",
        grid=(count,),
        out_shape=jax.ShapeDtypeStruct(queries.shape, BF16),
        in_specs=[SMEM, block] + [whole(own[0].shape)] * (2 * PARTS) + [kept] * len(filled),
        out_specs=block,
        scratch_shapes=[pltpu.VMEM((SHARDS * TOK, 2 * HD), BF16)],
        input_output_aliases={len(inputs) + k: k for k in range(len(filled))},
        compiler_params=pltpu.CompilerParams(vmem_limit_bytes=32 << 20),
        cost_estimate=pl.CostEstimate(
            flops=count << 30, bytes_accessed=4 << 20, transcendentals=count << 20
        ),
    )(*inputs, *filled)


def compose(earlier, later):
    return jnp.stack([earlier[0] * later[0], later[0] * earlier[1] + later[1]])


def near_prefix(couple, core):
    other = swapped(couple)
    first = core == 0
    inclusive = compose(jnp.where(first, couple, other), jnp.where(first, other, couple))
    empty = jnp.stack([jnp.ones_like(couple[0]), jnp.zeros_like(couple[0])])
    return jnp.where(first, empty, other), inclusive


def doubled(before, inclusive, arrived):
    return compose(arrived, before), compose(arrived, inclusive)


def shards(
    branch_in,
    branch_gate,
    conv_taps,
    conv_shift,
    inflow_weight,
    inflow_bias,
    decay_weight,
    decay_bias,
    decay_param,
    stream,
    norm_gain,
    memory_weight,
    queries,
):
    position = lax.axis_index(SEQ)
    core = lax.axis_index(CORE)
    turn = lax.axis_index("mp")
    place = turn.reshape(1)
    info = jnp.stack([core, position, turn]).astype(jnp.int32)
    line = lambda v: v.reshape(1, -1)

    edge = shifted(branch_in[TOK - (CONV - 1) :], 1)
    parts = project(place, stream, line(norm_gain), memory_weight)
    edge, *parts = lax.optimization_barrier((edge, *parts))
    arrived = [turned(parts[k], k) for k in range(1, PARTS)]
    rest = (
        branch_gate, conv_taps, line(conv_shift), inflow_weight, line(inflow_bias),
        decay_weight, line(decay_bias), line(decay_param),
    )
    groups = branch_in.shape[1] // BLK
    early = groups // 4
    filled = recur(0, early, branch_in, edge, *rest, ())
    own_part, *filled = lax.optimization_barrier((parts[0], *filled))
    quarter = normed([own_part] + arrived)
    trio = jnp.concatenate([quarter, shifted(quarter, 2), shifted(quarter, 4)])
    trio, edge = lax.optimization_barrier((trio, edge))
    own = [trio] + [turned(trio, k) for k in range(1, PARTS)]
    u, w, couple = recur(early, groups - early, branch_in, edge, *rest, filled)
    couple, *own = lax.optimization_barrier((couple, *own))
    before, inclusive = near_prefix(couple, core)
    before, inclusive = doubled(before, inclusive, shifted(inclusive, 2))
    other = [swapped(piece) for piece in own]
    before, inclusive = doubled(before, inclusive, shifted(inclusive, 4))
    heads = queries.shape[1] // HD
    half = heads // 2
    arrived = shifted(inclusive, 8)
    attended = attend(0, half, info, queries, own, other, ())
    arrived, attended = lax.optimization_barrier((arrived, attended))
    before, inclusive = doubled(before, inclusive, arrived)
    arrived = [shifted(inclusive, 16 * k) for k in range(1, 4)]
    attended = attend(half, heads - half, info, queries, own, other, (attended,))
    *arrived, attended = lax.optimization_barrier((*arrived, attended))
    for piece in arrived:
        before = compose(piece, before)
    recurrent_out = (u + w * before[1:2]).astype(BF16)
    return (recurrent_out, attended)


def solution(mesh):
    finer = Mesh(mesh.devices.reshape(8, 4, 2, mesh.shape["mp"]), (*SEQ, "mp"))
    in_specs = (
        P(SEQ, "mp"),
        P(SEQ, "mp"),
        P(None, "mp"),
        P("mp"),
        P("mp", None, None),
        P("mp"),
        P("mp", None, None),
        P("mp"),
        P("mp"),
        P(SEQ, "mp"),
        P("mp"),
        P("mp", None),
        P(SEQ, "mp"),
    )
    out_specs = (P(SEQ, "mp"), P(SEQ, "mp"))
    return jax.shard_map(
        shards, mesh=finer, in_specs=in_specs, out_specs=out_specs, check_vma=False
    )
```

```python
import functools

import jax
import jax.numpy as jnp
from jax import lax
from jax.experimental import pallas as pl
from jax.experimental.pallas import tpu as pltpu
from jax.sharding import Mesh
from jax.sharding import PartitionSpec as P

D = 4096
HD = 256
CONV = 4
WINDOW = 2048
BLK = 256
SEQ = ("seq_0", "seq_1", "seq_2")
CORE = "seq_2"
TOK = 512
QUARTER = 128
PARTS = 4
SEGMENTS = 8
STEPS = TOK // SEGMENTS
PITCH = STEPS + 1
QROWS = 256
LANES = 128
EXTRA = 16
ROOM = 60 << 20
SHARDS = 5

decay_power = 8.0
norm_epsilon = 1e-06
masked_score = -1e30
F32 = jnp.float32
BF16 = jnp.bfloat16
SMEM = pl.BlockSpec(memory_space=pltpu.SMEM)


def whole(shape):
    return pl.BlockSpec(shape, lambda *_: (0,) * len(shape))


def shifted(value, steps):
    count = lax.axis_size(SEQ)
    return lax.ppermute(value, SEQ, [(k, k + steps) for k in range(count - steps)])


def turned(value, steps):
    return lax.ppermute(value, "mp", [(k, (k + steps) % PARTS) for k in range(PARTS)])


def swapped(value):
    return lax.ppermute(value, CORE, [(0, 1), (1, 0)])


def project_kernel(place, stream, gain, weight, *parts):
    row = lax.broadcasted_iota(jnp.int32, (EXTRA, QUARTER), 0)
    for k, part in enumerate(parts):
        start = pl.multiple_of(lax.rem(place[0] + k, PARTS) * QUARTER, QUARTER)
        x = stream[pl.ds(start, QUARTER), :].astype(F32)
        squares = jnp.sum(x * x, axis=1, keepdims=True)
        scaled = (x * gain[...]).astype(BF16)
        product = jnp.dot(scaled, weight[...], preferred_element_type=F32)
        part[0:QUARTER, :] = product.astype(part.dtype)
        part[QUARTER:, :] = jnp.zeros((EXTRA, 2 * HD), part.dtype)
        line = jnp.broadcast_to(squares, (QUARTER, QUARTER)).T[0:EXTRA]
        high = line.astype(BF16).astype(F32)
        line = jnp.where(row == 0, high, jnp.where(row == 1, line - high, 0.0))
        part[QUARTER:, 0:QUARTER] = line.astype(part.dtype)


def project(place, stream, gain, weight):
    shape = (QUARTER + EXTRA, 2 * HD)
    return pl.pallas_call(
        project_kernel,
        name="project",
        out_shape=[jax.ShapeDtypeStruct(shape, F32 if k == 0 else BF16) for k in range(PARTS)],
        in_specs=[SMEM, whole(stream.shape), whole(gain.shape), whole(weight.shape)],
        out_specs=[whole(shape)] * PARTS,
        compiler_params=pltpu.CompilerParams(vmem_limit_bytes=ROOM),
        cost_estimate=pl.CostEstimate(flops=1 << 29, bytes_accessed=3 << 20, transcendentals=0),
    )(place, stream, gain, weight)


def split(value):
    high = value.astype(BF16).astype(F32)
    rest = value - high
    middle = rest.astype(BF16).astype(F32)
    return (high, middle, rest - middle)


def norm_kernel(info, a, b, c, d, couple, other, out, before, inclusive):
    total = (a[...] + b[...].astype(F32)) + (c[...].astype(F32) + d[...].astype(F32))
    line = total[QUARTER : QUARTER + 1, 0:QUARTER] + total[QUARTER + 1 : QUARTER + 2, 0:QUARTER]
    column = jnp.broadcast_to(line, (QUARTER, QUARTER)).T[:, 0:1]
    root = jnp.sqrt(column / D + norm_epsilon)
    out[0:QUARTER, :] = (total[0:QUARTER] / root).astype(BF16)
    first = info[0] == 0
    mine, theirs = (couple[...], other[...])
    earlier = jnp.where(first, mine, theirs)
    later = jnp.where(first, theirs, mine)
    factor = earlier[0:1] * later[0:1]
    state = later[0:1] * earlier[1:2] + later[1:2]
    inclusive[0:1, :] = factor
    inclusive[1:2, :] = state
    before[0:1, :] = jnp.where(first, jnp.ones_like(factor), theirs[0:1])
    before[1:2, :] = jnp.where(first, jnp.zeros_like(state), theirs[1:2])
    width = 2 * HD
    lines = [
        part[:, k : k + width]
        for value in (factor, state)
        for part in split(value)
        for k in range(0, value.shape[1], width)
    ]
    lines += [jnp.zeros((1, width), F32)] * (EXTRA - len(lines))
    out[QUARTER:, :] = jnp.concatenate(lines).astype(BF16)


def normed(info, parts, couple, other):
    shape = parts[0].shape
    return pl.pallas_call(
        norm_kernel,
        name="normed",
        out_shape=[
            jax.ShapeDtypeStruct(shape, BF16),
            jax.ShapeDtypeStruct(couple.shape, F32),
            jax.ShapeDtypeStruct(couple.shape, F32),
        ],
        in_specs=[SMEM] + [whole(shape)] * PARTS + [whole(couple.shape)] * 2,
        out_specs=[whole(shape), whole(couple.shape), whole(couple.shape)],
        compiler_params=pltpu.CompilerParams(vmem_limit_bytes=8 << 20),
        cost_estimate=pl.CostEstimate(flops=1 << 20, bytes_accessed=5 << 17, transcendentals=0),
    )(info, *parts, couple, other)


def received(lines, channels):
    values = []
    width = 2 * HD
    per = channels // width
    for value in range(2):
        halves = []
        for k in range(per):
            at = [value * 3 * per + part * per + k for part in range(3)]
            high, middle, low = [lines[row : row + 1] for row in at]
            halves.append(high + (middle + low))
        values.append(jnp.concatenate(halves, axis=1))
    return values


def window_kernel(mine, back2, back4, before, inclusive, trio, before_out, inclusive_out):
    channels = before.shape[1]
    passed = (before[0:1, :], before[1:2, :])
    whole_chip = (inclusive[0:1, :], inclusive[1:2, :])
    trio[0:QUARTER, :] = mine[0:QUARTER, :]
    for k, ref in enumerate((back2, back4)):
        trio[(k + 1) * QUARTER : (k + 2) * QUARTER, :] = ref[0:QUARTER, :]
        factor, state = received(ref[QUARTER:, :].astype(F32), channels)
        passed = (factor * passed[0], passed[0] * state + passed[1])
        whole_chip = (factor * whole_chip[0], whole_chip[0] * state + whole_chip[1])
    before_out[0:1, :], before_out[1:2, :] = passed
    inclusive_out[0:1, :], inclusive_out[1:2, :] = whole_chip


def window(mine, back2, back4, before, inclusive):
    shape = (3 * QUARTER, 2 * HD)
    couple = whole(before.shape)
    return pl.pallas_call(
        window_kernel,
        name="window",
        out_shape=[
            jax.ShapeDtypeStruct(shape, BF16),
            jax.ShapeDtypeStruct(before.shape, F32),
            jax.ShapeDtypeStruct(before.shape, F32),
        ],
        in_specs=[whole(mine.shape)] * 3 + [couple] * 2,
        out_specs=[whole(shape), couple, couple],
        compiler_params=pltpu.CompilerParams(vmem_limit_bytes=8 << 20),
        cost_estimate=pl.CostEstimate(flops=1 << 14, bytes_accessed=3 << 18, transcendentals=0),
    )(mine, back2, back4, before, inclusive)


def negative_expm1(y, grown):
    series = jnp.full_like(y, 1.0)
    for k in (8, 7, 6, 5, 4, 3, 2):
        series = 1.0 + series * (y * (1.0 / k))
    return jnp.where(y > -0.5, -y * series, 1.0 - grown)


def recur_kernel(
    branch, edge, gate, taps, shift, in_w, in_b, de_w, de_b, param, *rest
):
    u_out, w_out, end_out, extended, factors, pushes = rest[-6:]
    extended[8 : 8 + TOK, :] = branch[...].astype(F32)
    extended[8 - (CONV - 1) : 8, :] = edge[...].astype(F32)
    totals = shift[...] + taps[0:1, :] * extended[8 : 8 + TOK, :]
    for k in range(1, CONV):
        totals = totals + taps[k : k + 1, :] * extended[8 - k : 8 - k + TOK, :]
    mixed = totals.astype(BF16)
    inflow = jax.nn.sigmoid(
        jnp.dot(mixed, in_w[0], preferred_element_type=F32) + in_b[...]
    )
    recurrence = jax.nn.sigmoid(
        jnp.dot(mixed, de_w[0], preferred_element_type=F32) + de_b[...]
    )
    v = -param[...]
    soft = jnp.maximum(v, 0.0) + jnp.log1p(jnp.exp(-jnp.abs(v)))
    log_decay = recurrence * (-decay_power * soft)
    factor = jnp.exp(log_decay)
    push = (
        jnp.sqrt(negative_expm1(2.0 * log_decay, factor * factor))
        * inflow
        * mixed.astype(F32)
    )
    for lane in range(BLK // LANES):
        there = slice(lane * LANES, (lane + 1) * LANES)
        for r in range(SEGMENTS):
            rows = slice(r * STEPS, (r + 1) * STEPS)
            kept = slice(r * PITCH, r * PITCH + STEPS)
            factors[lane, kept, :] = factor[rows, there]
            pushes[lane, kept, :] = push[rows, there]

    lanes = range(BLK // LANES)
    product = [jnp.ones((SEGMENTS, LANES), F32) for _ in lanes]
    state = [jnp.zeros((SEGMENTS, LANES), F32) for _ in lanes]
    for t in range(STEPS):
        rows = pl.ds(t, SEGMENTS, stride=PITCH)
        for lane in lanes:
            f = factors[lane, rows, :]
            state[lane] = f * state[lane] + pushes[lane, rows, :]
            product[lane] = product[lane] * f
            pushes[lane, rows, :] = state[lane]
            factors[lane, rows, :] = product[lane]
    for lane in lanes:
        there = slice(lane * LANES, (lane + 1) * LANES)
        before_f = jnp.ones((1, LANES), F32)
        before_s = jnp.zeros((1, LANES), F32)
        for r in range(SEGMENTS):
            rows = slice(r * STEPS, (r + 1) * STEPS)
            g = gate[rows, there].astype(F32)
            g = 0.5 * g * (1.0 + jnp.tanh(0.7978845608028654 * (g + 0.044715 * (g * g * g))))
            kept = slice(r * PITCH, r * PITCH + STEPS)
            local_f = factors[lane, kept, :]
            u_out[rows, there] = (pushes[lane, kept, :] + local_f * before_s) * g
            w_out[rows, there] = (local_f * before_f) * g
            before_s = product[lane][r : r + 1] * before_s + state[lane][r : r + 1]
            before_f = product[lane][r : r + 1] * before_f
        end_out[0:1, there] = before_f
        end_out[1:2, there] = before_s


def recur(group, count, branch, edge, gate, taps, shift, in_w, in_b, de_w, de_b, param, filled):
    channels = branch.shape[1]
    lane = lambda rows: pl.BlockSpec((rows, BLK), lambda n: (0, n + group))
    square = pl.BlockSpec((1, BLK, BLK), lambda n: (n + group, 0, 0))
    kept = pl.BlockSpec(memory_space=pl.ANY)
    inputs = (branch, edge, gate, taps, shift, in_w, in_b, de_w, de_b, param)
    return pl.pallas_call(
        recur_kernel,
        name="recur",
        grid=(count,),
        out_shape=[
            jax.ShapeDtypeStruct((TOK, channels), F32),
            jax.ShapeDtypeStruct((TOK, channels), F32),
            jax.ShapeDtypeStruct((2, channels), F32),
        ],
        in_specs=[
            lane(TOK), lane(CONV - 1), lane(TOK), lane(CONV), lane(1),
            square, lane(1), square, lane(1), lane(1),
        ] + [kept] * len(filled),
        out_specs=[lane(TOK), lane(TOK), lane(2)],
        scratch_shapes=[
            pltpu.VMEM((TOK + 8, BLK), F32),
            pltpu.VMEM((BLK // LANES, SEGMENTS * PITCH, LANES), F32),
            pltpu.VMEM((BLK // LANES, SEGMENTS * PITCH, LANES), F32),
        ],
        input_output_aliases={len(inputs) + k: k for k in range(len(filled))},
        compiler_params=pltpu.CompilerParams(vmem_limit_bytes=ROOM),
        cost_estimate=pl.CostEstimate(
            flops=count << 28, bytes_accessed=count << 21, transcendentals=count << 20
        ),
    )(*inputs, *filled)


def attend_kernel(info, q_ref, *refs):
    own, other = (refs[0:PARTS], refs[PARTS : 2 * PARTS])
    out, kv = refs[-2:]
    core, position, place = (info[0], info[1], info[2])

    @pl.when(pl.program_id(0) == 0)
    def _():
        for k in range(PARTS):
            row = lax.rem(place + PARTS - k, PARTS) * QUARTER
            for behind in range(SHARDS):
                there = pl.ds(
                    pl.multiple_of((SHARDS - 1 - behind) * TOK + row, QUARTER), QUARTER
                )
                if behind % 2 == 0:
                    kv[there, :] = own[k][behind // 2 * QUARTER : (behind // 2 + 1) * QUARTER, :]
                else:
                    begin = pl.multiple_of(((behind + 1) // 2 - core) * QUARTER, QUARTER)
                    kv[there, :] = other[k][pl.ds(begin, QUARTER), :]

    def bias(behind):
        return jnp.where(position >= behind, 0.0, masked_score).astype(F32)

    rows = lax.broadcasted_iota(jnp.int32, (QROWS, QROWS), 0)
    columns = lax.broadcasted_iota(jnp.int32, (QROWS, QROWS), 1)
    causal = rows >= columns
    last = (SHARDS - 1) * TOK
    for half in range(2):
        low = half * QROWS
        q = q_ref[low : low + QROWS, :] * jnp.asarray(HD**-0.5, BF16)
        blocks = [(k * TOK, TOK, bias(SHARDS - 1 - k), None) for k in range(1, SHARDS - 1)]
        if half == 0:
            blocks.append((QROWS, QROWS, bias(SHARDS - 1), None))
        else:
            blocks.append((last, QROWS, None, None))
        blocks.append((low, QROWS, bias(SHARDS - 1), ~causal))
        blocks.append((last + low, QROWS, None, causal))
        scores = []
        for begin, size, extra, mask in blocks:
            s = lax.dot_general(
                q,
                kv[begin : begin + size, 0:HD],
                (((1,), (1,)), ((), ())),
                preferred_element_type=F32,
            )
            if extra is not None:
                s = s + extra
            if mask is not None:
                s = jnp.where(mask, s, masked_score)
            scores.append(s)
        tiles = [s[:, k : k + 128] for s in scores for k in range(0, s.shape[1], 128)]
        peak = jnp.max(functools.reduce(jnp.maximum, tiles), axis=1, keepdims=True)
        weights = [jnp.exp(s - peak) for s in scores]
        tiles = [p[:, k : k + 128] for p in weights for k in range(0, p.shape[1], 128)]
        norm = jnp.sum(functools.reduce(jnp.add, tiles), axis=1, keepdims=True)
        total = jnp.zeros((QROWS, HD), F32)
        for p, (begin, size, _, _) in zip(weights, blocks):
            total = total + jnp.dot(
                p.astype(BF16), kv[begin : begin + size, HD:], preferred_element_type=F32
            )
        out[low : low + QROWS, :] = (total / norm).astype(BF16)


def attend(head, count, info, queries, own, other, filled):
    block = pl.BlockSpec((TOK, HD), lambda h: (0, h + head))
    kept = pl.BlockSpec(memory_space=pl.ANY)
    inputs = (info, queries, *own, *other)
    return pl.pallas_call(
        attend_kernel,
        name="attend",
        grid=(count,),
        out_shape=jax.ShapeDtypeStruct(queries.shape, BF16),
        in_specs=[SMEM, block] + [whole(own[0].shape)] * (2 * PARTS) + [kept] * len(filled),
        out_specs=block,
        scratch_shapes=[pltpu.VMEM((SHARDS * TOK, 2 * HD), BF16)],
        input_output_aliases={len(inputs) + k: k for k in range(len(filled))},
        compiler_params=pltpu.CompilerParams(vmem_limit_bytes=32 << 20),
        cost_estimate=pl.CostEstimate(
            flops=count << 30, bytes_accessed=4 << 20, transcendentals=count << 20
        ),
    )(*inputs, *filled)


def compose(earlier, later):
    return jnp.stack([earlier[0] * later[0], later[0] * earlier[1] + later[1]])


def shards(
    branch_in,
    branch_gate,
    conv_taps,
    conv_shift,
    inflow_weight,
    inflow_bias,
    decay_weight,
    decay_bias,
    decay_param,
    stream,
    norm_gain,
    memory_weight,
    queries,
):
    position = lax.axis_index(SEQ)
    core = lax.axis_index(CORE)
    turn = lax.axis_index("mp")
    place = turn.reshape(1)
    info = jnp.stack([core, position, turn]).astype(jnp.int32)
    line = lambda v: v.reshape(1, -1)

    edge = shifted(branch_in[TOK - (CONV - 1) :], 1)
    parts = project(place, stream, line(norm_gain), memory_weight)
    edge, *parts = lax.optimization_barrier((edge, *parts))
    arrived = [turned(parts[k], k) for k in range(1, PARTS)]
    rest = (
        branch_gate, conv_taps, line(conv_shift), inflow_weight, line(inflow_bias),
        decay_weight, line(decay_bias), line(decay_param),
    )
    groups = branch_in.shape[1] // BLK
    u, w, couple = recur(0, groups, branch_in, edge, *rest, ())
    mine, before, inclusive = normed(info, [parts[0]] + arrived, couple, swapped(couple))
    trio, before, inclusive = window(
        mine, shifted(mine, 2), shifted(mine, 4), before, inclusive
    )
    own = [trio] + [turned(trio, k) for k in range(1, PARTS)]
    far = [shifted(inclusive, 6 * k) for k in (1, 2, 3)]
    *far, own[1], own[2], own[3] = lax.optimization_barrier((*far, *own[1:]))
    for couple in far:
        before = compose(couple, before)
        inclusive = compose(couple, inclusive)
    other = [swapped(piece) for piece in own]
    far = [shifted(inclusive, 24 * k) for k in (1, 2)]
    heads = queries.shape[1] // HD
    attended = attend(0, heads, info, queries, own, other, ())
    *far, attended = lax.optimization_barrier((*far, attended))
    for couple in far:
        before = compose(couple, before)
    recurrent_out = (u + w * before[1:2]).astype(BF16)
    return (recurrent_out, attended)


def solution(mesh):
    finer = Mesh(mesh.devices.reshape(8, 4, 2, mesh.shape["mp"]), (*SEQ, "mp"))
    in_specs = (
        P(SEQ, "mp"),
        P(SEQ, "mp"),
        P(None, "mp"),
        P("mp"),
        P("mp", None, None),
        P("mp"),
        P("mp", None, None),
        P("mp"),
        P("mp"),
        P(SEQ, "mp"),
        P("mp"),
        P("mp", None),
        P(SEQ, "mp"),
    )
    out_specs = (P(SEQ, "mp"), P(SEQ, "mp"))
    return jax.shard_map(
        shards, mesh=finer, in_specs=in_specs, out_specs=out_specs, check_vma=False
    )
```

```python
import functools

import jax
import jax.numpy as jnp
from jax import lax
from jax.experimental import pallas as pl
from jax.experimental.pallas import tpu as pltpu
from jax.sharding import Mesh
from jax.sharding import PartitionSpec as P

D = 4096
HD = 256
CONV = 4
WINDOW = 2048
BLK = 256
SEQ = ("seq_0", "seq_1", "seq_2")
CORE = "seq_2"
TOK = 512
QUARTER = 128
PARTS = 4
SEGMENTS = 8
STEPS = TOK // SEGMENTS
PITCH = STEPS + 1
QROWS = 256
LANES = 128
EXTRA = 16
ROOM = 60 << 20
SHARDS = 5

decay_power = 8.0
norm_epsilon = 1e-06
masked_score = -1e30
F32 = jnp.float32
BF16 = jnp.bfloat16
SMEM = pl.BlockSpec(memory_space=pltpu.SMEM)


def whole(shape):
    return pl.BlockSpec(shape, lambda *_: (0,) * len(shape))


def shifted(value, steps):
    count = lax.axis_size(SEQ)
    return lax.ppermute(value, SEQ, [(k, k + steps) for k in range(count - steps)])


def turned(value, steps):
    return lax.ppermute(value, "mp", [(k, (k + steps) % PARTS) for k in range(PARTS)])


def swapped(value):
    return lax.ppermute(value, CORE, [(0, 1), (1, 0)])


def project_kernel(place, stream, gain, weight, *parts):
    row = lax.broadcasted_iota(jnp.int32, (EXTRA, QUARTER), 0)
    for k, part in enumerate(parts):
        start = pl.multiple_of(lax.rem(place[0] + k, PARTS) * QUARTER, QUARTER)
        x = stream[pl.ds(start, QUARTER), :].astype(F32)
        squares = jnp.sum(x * x, axis=1, keepdims=True)
        scaled = (x * gain[...]).astype(BF16)
        product = jnp.dot(scaled, weight[...], preferred_element_type=F32)
        part[0:QUARTER, :] = product.astype(part.dtype)
        part[QUARTER:, :] = jnp.zeros((EXTRA, 2 * HD), part.dtype)
        line = jnp.broadcast_to(squares, (QUARTER, QUARTER)).T[0:EXTRA]
        high = line.astype(BF16).astype(F32)
        line = jnp.where(row == 0, high, jnp.where(row == 1, line - high, 0.0))
        part[QUARTER:, 0:QUARTER] = line.astype(part.dtype)


def project(place, stream, gain, weight):
    shape = (QUARTER + EXTRA, 2 * HD)
    return pl.pallas_call(
        project_kernel,
        name="project",
        out_shape=[jax.ShapeDtypeStruct(shape, F32 if k == 0 else BF16) for k in range(PARTS)],
        in_specs=[SMEM, whole(stream.shape), whole(gain.shape), whole(weight.shape)],
        out_specs=[whole(shape)] * PARTS,
        compiler_params=pltpu.CompilerParams(vmem_limit_bytes=ROOM),
        cost_estimate=pl.CostEstimate(flops=1 << 29, bytes_accessed=3 << 20, transcendentals=0),
    )(place, stream, gain, weight)


def split(value):
    high = value.astype(BF16).astype(F32)
    rest = value - high
    middle = rest.astype(BF16).astype(F32)
    return (high, middle, rest - middle)


def norm_kernel(info, a, b, c, d, couple, other, out, before, inclusive):
    total = (a[...] + b[...].astype(F32)) + (c[...].astype(F32) + d[...].astype(F32))
    line = total[QUARTER : QUARTER + 1, 0:QUARTER] + total[QUARTER + 1 : QUARTER + 2, 0:QUARTER]
    column = jnp.broadcast_to(line, (QUARTER, QUARTER)).T[:, 0:1]
    root = jnp.sqrt(column / D + norm_epsilon)
    out[0:QUARTER, :] = (total[0:QUARTER] / root).astype(BF16)
    first = info[0] == 0
    mine, theirs = (couple[...], other[...])
    earlier = jnp.where(first, mine, theirs)
    later = jnp.where(first, theirs, mine)
    factor = earlier[0:1] * later[0:1]
    state = later[0:1] * earlier[1:2] + later[1:2]
    inclusive[0:1, :] = factor
    inclusive[1:2, :] = state
    before[0:1, :] = jnp.where(first, jnp.ones_like(factor), theirs[0:1])
    before[1:2, :] = jnp.where(first, jnp.zeros_like(state), theirs[1:2])
    width = 2 * HD
    lines = [
        part[:, k : k + width]
        for value in (factor, state)
        for part in split(value)
        for k in range(0, value.shape[1], width)
    ]
    lines += [jnp.zeros((1, width), F32)] * (EXTRA - len(lines))
    out[QUARTER:, :] = jnp.concatenate(lines).astype(BF16)


def normed(info, parts, couple, other):
    shape = parts[0].shape
    return pl.pallas_call(
        norm_kernel,
        name="normed",
        out_shape=[
            jax.ShapeDtypeStruct(shape, BF16),
            jax.ShapeDtypeStruct(couple.shape, F32),
            jax.ShapeDtypeStruct(couple.shape, F32),
        ],
        in_specs=[SMEM] + [whole(shape)] * PARTS + [whole(couple.shape)] * 2,
        out_specs=[whole(shape), whole(couple.shape), whole(couple.shape)],
        compiler_params=pltpu.CompilerParams(vmem_limit_bytes=8 << 20),
        cost_estimate=pl.CostEstimate(flops=1 << 20, bytes_accessed=5 << 17, transcendentals=0),
    )(info, *parts, couple, other)


def received(lines, channels):
    values = []
    width = 2 * HD
    per = channels // width
    for value in range(2):
        halves = []
        for k in range(per):
            at = [value * 3 * per + part * per + k for part in range(3)]
            high, middle, low = [lines[row : row + 1] for row in at]
            halves.append(high + (middle + low))
        values.append(jnp.concatenate(halves, axis=1))
    return values


def window_kernel(mine, back2, back4, before, inclusive, trio, before_out, inclusive_out):
    channels = before.shape[1]
    passed = (before[0:1, :], before[1:2, :])
    whole_chip = (inclusive[0:1, :], inclusive[1:2, :])
    trio[0:QUARTER, :] = mine[0:QUARTER, :]
    for k, ref in enumerate((back2, back4)):
        trio[(k + 1) * QUARTER : (k + 2) * QUARTER, :] = ref[0:QUARTER, :]
        factor, state = received(ref[QUARTER:, :].astype(F32), channels)
        passed = (factor * passed[0], passed[0] * state + passed[1])
        whole_chip = (factor * whole_chip[0], whole_chip[0] * state + whole_chip[1])
    before_out[0:1, :], before_out[1:2, :] = passed
    inclusive_out[0:1, :], inclusive_out[1:2, :] = whole_chip


def window(mine, back2, back4, before, inclusive):
    shape = (3 * QUARTER, 2 * HD)
    couple = whole(before.shape)
    return pl.pallas_call(
        window_kernel,
        name="window",
        out_shape=[
            jax.ShapeDtypeStruct(shape, BF16),
            jax.ShapeDtypeStruct(before.shape, F32),
            jax.ShapeDtypeStruct(before.shape, F32),
        ],
        in_specs=[whole(mine.shape)] * 3 + [couple] * 2,
        out_specs=[whole(shape), couple, couple],
        compiler_params=pltpu.CompilerParams(vmem_limit_bytes=8 << 20),
        cost_estimate=pl.CostEstimate(flops=1 << 14, bytes_accessed=3 << 18, transcendentals=0),
    )(mine, back2, back4, before, inclusive)


def negative_expm1(y, grown):
    series = jnp.full_like(y, 1.0)
    for k in (8, 7, 6, 5, 4, 3, 2):
        series = 1.0 + series * (y * (1.0 / k))
    return jnp.where(y > -0.5, -y * series, 1.0 - grown)


def recur_kernel(
    branch, edge, gate, taps, shift, in_w, in_b, de_w, de_b, param, *rest
):
    u_out, w_out, end_out, extended, factors, pushes = rest[-6:]
    extended[8 : 8 + TOK, :] = branch[...].astype(F32)
    extended[8 - (CONV - 1) : 8, :] = edge[...].astype(F32)
    totals = shift[...] + taps[0:1, :] * extended[8 : 8 + TOK, :]
    for k in range(1, CONV):
        totals = totals + taps[k : k + 1, :] * extended[8 - k : 8 - k + TOK, :]
    mixed = totals.astype(BF16)
    inflow = jax.nn.sigmoid(
        jnp.dot(mixed, in_w[0], preferred_element_type=F32) + in_b[...]
    )
    recurrence = jax.nn.sigmoid(
        jnp.dot(mixed, de_w[0], preferred_element_type=F32) + de_b[...]
    )
    v = -param[...]
    soft = jnp.maximum(v, 0.0) + jnp.log1p(jnp.exp(-jnp.abs(v)))
    log_decay = recurrence * (-decay_power * soft)
    factor = jnp.exp(log_decay)
    push = (
        jnp.sqrt(negative_expm1(2.0 * log_decay, factor * factor))
        * inflow
        * mixed.astype(F32)
    )
    for lane in range(BLK // LANES):
        there = slice(lane * LANES, (lane + 1) * LANES)
        for r in range(SEGMENTS):
            rows = slice(r * STEPS, (r + 1) * STEPS)
            kept = slice(r * PITCH, r * PITCH + STEPS)
            factors[lane, kept, :] = factor[rows, there]
            pushes[lane, kept, :] = push[rows, there]

    lanes = range(BLK // LANES)
    product = [jnp.ones((SEGMENTS, LANES), F32) for _ in lanes]
    state = [jnp.zeros((SEGMENTS, LANES), F32) for _ in lanes]
    for t in range(STEPS):
        rows = pl.ds(t, SEGMENTS, stride=PITCH)
        for lane in lanes:
            f = factors[lane, rows, :]
            state[lane] = f * state[lane] + pushes[lane, rows, :]
            product[lane] = product[lane] * f
            pushes[lane, rows, :] = state[lane]
            factors[lane, rows, :] = product[lane]
    for lane in lanes:
        there = slice(lane * LANES, (lane + 1) * LANES)
        before_f = jnp.ones((1, LANES), F32)
        before_s = jnp.zeros((1, LANES), F32)
        for r in range(SEGMENTS):
            rows = slice(r * STEPS, (r + 1) * STEPS)
            g = gate[rows, there].astype(F32)
            g = 0.5 * g * (1.0 + jnp.tanh(0.7978845608028654 * (g + 0.044715 * (g * g * g))))
            kept = slice(r * PITCH, r * PITCH + STEPS)
            local_f = factors[lane, kept, :]
            u_out[rows, there] = (pushes[lane, kept, :] + local_f * before_s) * g
            w_out[rows, there] = (local_f * before_f) * g
            before_s = product[lane][r : r + 1] * before_s + state[lane][r : r + 1]
            before_f = product[lane][r : r + 1] * before_f
        end_out[0:1, there] = before_f
        end_out[1:2, there] = before_s


def recur(group, count, branch, edge, gate, taps, shift, in_w, in_b, de_w, de_b, param, filled):
    channels = branch.shape[1]
    lane = lambda rows: pl.BlockSpec((rows, BLK), lambda n: (0, n + group))
    square = pl.BlockSpec((1, BLK, BLK), lambda n: (n + group, 0, 0))
    kept = pl.BlockSpec(memory_space=pl.ANY)
    inputs = (branch, edge, gate, taps, shift, in_w, in_b, de_w, de_b, param)
    return pl.pallas_call(
        recur_kernel,
        name="recur",
        grid=(count,),
        out_shape=[
            jax.ShapeDtypeStruct((TOK, channels), F32),
            jax.ShapeDtypeStruct((TOK, channels), F32),
            jax.ShapeDtypeStruct((2, channels), F32),
        ],
        in_specs=[
            lane(TOK), lane(CONV - 1), lane(TOK), lane(CONV), lane(1),
            square, lane(1), square, lane(1), lane(1),
        ] + [kept] * len(filled),
        out_specs=[lane(TOK), lane(TOK), lane(2)],
        scratch_shapes=[
            pltpu.VMEM((TOK + 8, BLK), F32),
            pltpu.VMEM((BLK // LANES, SEGMENTS * PITCH, LANES), F32),
            pltpu.VMEM((BLK // LANES, SEGMENTS * PITCH, LANES), F32),
        ],
        input_output_aliases={len(inputs) + k: k for k in range(len(filled))},
        compiler_params=pltpu.CompilerParams(vmem_limit_bytes=ROOM),
        cost_estimate=pl.CostEstimate(
            flops=count << 28, bytes_accessed=count << 21, transcendentals=count << 20
        ),
    )(*inputs, *filled)


def attend_head(q_ref, kv, out, admitted):
    def scored(q, begin, size):
        return lax.dot_general(
            q,
            kv[begin : begin + size, 0:HD],
            (((1,), (1,)), ((), ())),
            preferred_element_type=F32,
        )

    rows = lax.broadcasted_iota(jnp.int32, (QROWS, QROWS), 0)
    columns = lax.broadcasted_iota(jnp.int32, (QROWS, QROWS), 1)
    causal = rows >= columns
    last = (SHARDS - 1) * TOK
    q = q_ref[...] * jnp.asarray(HD**-0.5, BF16)
    most = SHARDS - 1
    wide = [admitted(scored(q, k * TOK, TOK), most - k) for k in range(1, most)]
    for half in range(2):
        low = half * QROWS
        rows = slice(low, low + QROWS)
        far = admitted(scored(q[rows], low, QROWS), most)
        near = scored(q[rows], last + low, QROWS)
        blocks = [(k * TOK, s[rows]) for k, s in zip(range(1, SHARDS - 1), wide)]
        blocks.append((low, jnp.where(causal, masked_score, far)))
        blocks.append((last + low, jnp.where(causal, near, masked_score)))
        if half == 0:
            blocks.append((QROWS, admitted(scored(q[rows], QROWS, QROWS), most)))
        else:
            blocks.append((last, scored(q[rows], last, QROWS)))
        tiles = [s[:, k : k + 128] for _, s in blocks for k in range(0, s.shape[1], 128)]
        peak = jnp.max(functools.reduce(jnp.maximum, tiles), axis=1, keepdims=True)
        weights = [jnp.exp(s - peak) for _, s in blocks]
        tiles = [p[:, k : k + 128] for p in weights for k in range(0, p.shape[1], 128)]
        norm = jnp.sum(functools.reduce(jnp.add, tiles), axis=1, keepdims=True)
        total = jnp.zeros((QROWS, HD), F32)
        for p, (begin, _) in zip(weights, blocks):
            total = total + jnp.dot(
                p.astype(BF16),
                kv[begin : begin + p.shape[1], HD:],
                preferred_element_type=F32,
            )
        out[rows, :] = (total / norm).astype(BF16)


def attend_kernel(info, q_ref, *refs):
    own, other = (refs[0:PARTS], refs[PARTS : 2 * PARTS])
    out, kv = refs[-2:]
    core, position, place = (info[0], info[1], info[2])

    @pl.when(pl.program_id(0) == 0)
    def _():
        for k in range(PARTS):
            row = lax.rem(place + PARTS - k, PARTS) * QUARTER
            for behind in range(SHARDS):
                there = pl.ds(
                    pl.multiple_of((SHARDS - 1 - behind) * TOK + row, QUARTER), QUARTER
                )
                if behind % 2 == 0:
                    kv[there, :] = own[k][behind // 2 * QUARTER : (behind // 2 + 1) * QUARTER, :]
                else:
                    begin = pl.multiple_of(((behind + 1) // 2 - core) * QUARTER, QUARTER)
                    kv[there, :] = other[k][pl.ds(begin, QUARTER), :]

    @pl.when(position >= SHARDS - 1)
    def _():
        attend_head(q_ref, kv, out, lambda s, behind: s)

    @pl.when(position < SHARDS - 1)
    def _():
        attend_head(
            q_ref, kv, out, lambda s, behind: jnp.where(position >= behind, s, masked_score)
        )


def attend(head, count, info, queries, own, other, filled):
    block = pl.BlockSpec((TOK, HD), lambda h: (0, h + head))
    kept = pl.BlockSpec(memory_space=pl.ANY)
    inputs = (info, queries, *own, *other)
    return pl.pallas_call(
        attend_kernel,
        name="attend",
        grid=(count,),
        out_shape=jax.ShapeDtypeStruct(queries.shape, BF16),
        in_specs=[SMEM, block] + [whole(own[0].shape)] * (2 * PARTS) + [kept] * len(filled),
        out_specs=block,
        scratch_shapes=[pltpu.VMEM((SHARDS * TOK, 2 * HD), BF16)],
        input_output_aliases={len(inputs) + k: k for k in range(len(filled))},
        compiler_params=pltpu.CompilerParams(vmem_limit_bytes=32 << 20),
        cost_estimate=pl.CostEstimate(
            flops=count << 30, bytes_accessed=4 << 20, transcendentals=count << 20
        ),
    )(*inputs, *filled)


def compose(earlier, later):
    return jnp.stack([earlier[0] * later[0], later[0] * earlier[1] + later[1]])


def shards(
    branch_in,
    branch_gate,
    conv_taps,
    conv_shift,
    inflow_weight,
    inflow_bias,
    decay_weight,
    decay_bias,
    decay_param,
    stream,
    norm_gain,
    memory_weight,
    queries,
):
    position = lax.axis_index(SEQ)
    core = lax.axis_index(CORE)
    turn = lax.axis_index("mp")
    place = turn.reshape(1)
    info = jnp.stack([core, position, turn]).astype(jnp.int32)
    line = lambda v: v.reshape(1, -1)

    edge = shifted(branch_in[TOK - (CONV - 1) :], 1)
    parts = project(place, stream, line(norm_gain), memory_weight)
    edge, *parts = lax.optimization_barrier((edge, *parts))
    arrived = [turned(parts[k], k) for k in range(1, PARTS)]
    rest = (
        branch_gate, conv_taps, line(conv_shift), inflow_weight, line(inflow_bias),
        decay_weight, line(decay_bias), line(decay_param),
    )
    groups = branch_in.shape[1] // BLK
    u, w, couple = recur(0, groups, branch_in, edge, *rest, ())
    mine, before, inclusive = normed(info, [parts[0]] + arrived, couple, swapped(couple))
    trio, before, inclusive = window(
        mine, shifted(mine, 2), shifted(mine, 4), before, inclusive
    )
    own = [trio] + [turned(trio, k) for k in range(1, PARTS)]
    far = [shifted(inclusive, 6 * k) for k in (1, 2)]
    *far, own[1], own[2], own[3] = lax.optimization_barrier((*far, *own[1:]))
    for couple in far:
        before = compose(couple, before)
        inclusive = compose(couple, inclusive)
    other = [swapped(piece) for piece in own]
    far = [shifted(inclusive, 18 * k) for k in (1, 2, 3)]
    heads = queries.shape[1] // HD
    attended = attend(0, heads, info, queries, own, other, ())
    *far, attended = lax.optimization_barrier((*far, attended))
    for couple in far:
        before = compose(couple, before)
    recurrent_out = (u + w * before[1:2]).astype(BF16)
    return (recurrent_out, attended)


def solution(mesh):
    finer = Mesh(mesh.devices.reshape(8, 4, 2, mesh.shape["mp"]), (*SEQ, "mp"))
    in_specs = (
        P(SEQ, "mp"),
        P(SEQ, "mp"),
        P(None, "mp"),
        P("mp"),
        P("mp", None, None),
        P("mp"),
        P("mp", None, None),
        P("mp"),
        P("mp"),
        P(SEQ, "mp"),
        P("mp"),
        P("mp", None),
        P(SEQ, "mp"),
    )
    out_specs = (P(SEQ, "mp"), P(SEQ, "mp"))
    return jax.shard_map(
        shards, mesh=finer, in_specs=in_specs, out_specs=out_specs, check_vma=False
    )
```

```python
import functools

import jax
import jax.numpy as jnp
from jax import lax
from jax.experimental import pallas as pl
from jax.experimental.pallas import tpu as pltpu
from jax.sharding import Mesh
from jax.sharding import PartitionSpec as P

D = 4096
HD = 256
CONV = 4
WINDOW = 2048
BLK = 256
SEQ = ("seq_0", "seq_1", "seq_2")
CORE = "seq_2"
TOK = 512
QUARTER = 128
PARTS = 4
SEGMENTS = 8
STEPS = TOK // SEGMENTS
PITCH = STEPS + 1
QROWS = 256
LANES = 128
EXTRA = 16
ROOM = 60 << 20
SHARDS = 5

decay_power = 8.0
norm_epsilon = 1e-06
masked_score = -1e30
F32 = jnp.float32
BF16 = jnp.bfloat16
SMEM = pl.BlockSpec(memory_space=pltpu.SMEM)


def whole(shape):
    return pl.BlockSpec(shape, lambda *_: (0,) * len(shape))


def shifted(value, steps):
    count = lax.axis_size(SEQ)
    return lax.ppermute(value, SEQ, [(k, k + steps) for k in range(count - steps)])


def forked(value, near, distant):
    chips = lax.axis_size(SEQ) // 2
    pairs = [(2 * c, 2 * (c + near)) for c in range(chips - near)]
    pairs += [(2 * c + 1, 2 * (c + distant) + 1) for c in range(chips - distant)]
    return lax.ppermute(value, SEQ, pairs)


def turned(value, steps):
    return lax.ppermute(value, "mp", [(k, (k + steps) % PARTS) for k in range(PARTS)])


def swapped(value):
    return lax.ppermute(value, CORE, [(0, 1), (1, 0)])


def project_kernel(place, stream, gain, weight, *parts):
    row = lax.broadcasted_iota(jnp.int32, (EXTRA, QUARTER), 0)
    for k, part in enumerate(parts):
        start = pl.multiple_of(lax.rem(place[0] + k, PARTS) * QUARTER, QUARTER)
        x = stream[pl.ds(start, QUARTER), :].astype(F32)
        squares = jnp.sum(x * x, axis=1, keepdims=True)
        scaled = (x * gain[...]).astype(BF16)
        product = jnp.dot(scaled, weight[...], preferred_element_type=F32)
        part[0:QUARTER, :] = product.astype(part.dtype)
        part[QUARTER:, :] = jnp.zeros((EXTRA, 2 * HD), part.dtype)
        line = jnp.broadcast_to(squares, (QUARTER, QUARTER)).T[0:EXTRA]
        high = line.astype(BF16).astype(F32)
        line = jnp.where(row == 0, high, jnp.where(row == 1, line - high, 0.0))
        part[QUARTER:, 0:QUARTER] = line.astype(part.dtype)


def project(place, stream, gain, weight):
    shape = (QUARTER + EXTRA, 2 * HD)
    return pl.pallas_call(
        project_kernel,
        name="project",
        out_shape=[jax.ShapeDtypeStruct(shape, F32 if k == 0 else BF16) for k in range(PARTS)],
        in_specs=[SMEM, whole(stream.shape), whole(gain.shape), whole(weight.shape)],
        out_specs=[whole(shape)] * PARTS,
        compiler_params=pltpu.CompilerParams(vmem_limit_bytes=ROOM),
        cost_estimate=pl.CostEstimate(flops=1 << 29, bytes_accessed=3 << 20, transcendentals=0),
    )(place, stream, gain, weight)


def split(value):
    high = value.astype(BF16).astype(F32)
    rest = value - high
    middle = rest.astype(BF16).astype(F32)
    return (high, middle, rest - middle)


def norm_kernel(a, b, c, d, couple, out):
    total = (a[...] + b[...].astype(F32)) + (c[...].astype(F32) + d[...].astype(F32))
    line = total[QUARTER : QUARTER + 1, 0:QUARTER] + total[QUARTER + 1 : QUARTER + 2, 0:QUARTER]
    column = jnp.broadcast_to(line, (QUARTER, QUARTER)).T[:, 0:1]
    root = jnp.sqrt(column / D + norm_epsilon)
    out[0:QUARTER, :] = (total[0:QUARTER] / root).astype(BF16)
    width = 2 * HD
    lines = [
        part[:, k : k + width]
        for value in (couple[0:1, :], couple[1:2, :])
        for part in split(value)
        for k in range(0, value.shape[1], width)
    ]
    lines += [jnp.zeros((1, width), F32)] * (EXTRA - len(lines))
    out[QUARTER:, :] = jnp.concatenate(lines).astype(BF16)


def normed(parts, couple):
    shape = parts[0].shape
    return pl.pallas_call(
        norm_kernel,
        name="normed",
        out_shape=jax.ShapeDtypeStruct(shape, BF16),
        in_specs=[whole(shape)] * PARTS + [whole(couple.shape)],
        out_specs=whole(shape),
        compiler_params=pltpu.CompilerParams(vmem_limit_bytes=8 << 20),
        cost_estimate=pl.CostEstimate(flops=1 << 20, bytes_accessed=5 << 17, transcendentals=0),
    )(*parts, couple)


def received(lines, channels):
    values = []
    width = 2 * HD
    per = channels // width
    for value in range(2):
        halves = []
        for k in range(per):
            at = [value * 3 * per + part * per + k for part in range(3)]
            high, middle, low = [lines[row : row + 1] for row in at]
            halves.append(high + (middle + low))
        values.append(jnp.concatenate(halves, axis=1))
    return values


def applied(earlier, later):
    return (earlier[0] * later[0], later[0] * earlier[1] + later[1])


def chosen(flag, first, second):
    return [jnp.where(flag, x, y) for x, y in zip(first, second)]


def window_kernel(info, pair, arrived, trio, before, inclusive, got):
    channels = before.shape[1]
    first = info[0] == 0
    each = QUARTER + EXTRA
    trio[0:QUARTER, :] = pair[0:QUARTER, :]
    trio[QUARTER : 2 * QUARTER, :] = arrived[0:QUARTER, :]
    trio[2 * QUARTER :, :] = arrived[each : each + QUARTER, :]
    for ref, out in ((pair, inclusive), (arrived, got)):
        mine = received(ref[QUARTER:each, :].astype(F32), channels)
        theirs = received(ref[each + QUARTER :, :].astype(F32), channels)
        chip = applied(chosen(first, mine, theirs), chosen(first, theirs, mine))
        out[0:1, :], out[1:2, :] = chip
        if ref is pair:
            none = (jnp.ones_like(theirs[0]), jnp.zeros_like(theirs[1]))
            before[0:1, :], before[1:2, :] = chosen(first, none, theirs)


def window(info, pair, arrived, channels):
    shape = (3 * QUARTER, 2 * HD)
    couple = (2, channels)
    return pl.pallas_call(
        window_kernel,
        name="window",
        out_shape=[jax.ShapeDtypeStruct(shape, BF16)] + [jax.ShapeDtypeStruct(couple, F32)] * 3,
        in_specs=[SMEM] + [whole(pair.shape)] * 2,
        out_specs=[whole(shape)] + [whole(couple)] * 3,
        compiler_params=pltpu.CompilerParams(vmem_limit_bytes=8 << 20),
        cost_estimate=pl.CostEstimate(flops=1 << 14, bytes_accessed=3 << 18, transcendentals=0),
    )(info, pair, arrived)


def merge_kernel(info, before, inclusive, mine, theirs, before_out, inclusive_out):
    first = info[0] == 0
    passed = (before[0:1, :], before[1:2, :])
    covered = (inclusive[0:1, :], inclusive[1:2, :])
    for at in range(0, mine.shape[0], 2):
        ours = (mine[at : at + 1, :], mine[at + 1 : at + 2, :])
        other = (theirs[at : at + 1, :], theirs[at + 1 : at + 2, :])
        for earlier in (chosen(first, ours, other), chosen(first, other, ours)):
            passed = applied(earlier, passed)
            covered = applied(earlier, covered)
    before_out[0:1, :], before_out[1:2, :] = passed
    inclusive_out[0:1, :], inclusive_out[1:2, :] = covered


def merged(info, before, inclusive, mine, theirs):
    couple = whole(before.shape)
    return pl.pallas_call(
        merge_kernel,
        name="merged",
        out_shape=[jax.ShapeDtypeStruct(before.shape, F32)] * 2,
        in_specs=[SMEM, couple, couple, whole(mine.shape), whole(mine.shape)],
        out_specs=[couple, couple],
        compiler_params=pltpu.CompilerParams(vmem_limit_bytes=4 << 20),
        cost_estimate=pl.CostEstimate(flops=1 << 14, bytes_accessed=1 << 16, transcendentals=0),
    )(info, before, inclusive, mine, theirs)


def negative_expm1(y, grown):
    series = jnp.full_like(y, 1.0)
    for k in (8, 7, 6, 5, 4, 3, 2):
        series = 1.0 + series * (y * (1.0 / k))
    return jnp.where(y > -0.5, -y * series, 1.0 - grown)


def recur_kernel(
    branch, edge, gate, taps, shift, in_w, in_b, de_w, de_b, param, *rest
):
    u_out, w_out, end_out, extended, factors, pushes = rest[-6:]
    extended[8 : 8 + TOK, :] = branch[...].astype(F32)
    extended[8 - (CONV - 1) : 8, :] = edge[...].astype(F32)
    totals = shift[...] + taps[0:1, :] * extended[8 : 8 + TOK, :]
    for k in range(1, CONV):
        totals = totals + taps[k : k + 1, :] * extended[8 - k : 8 - k + TOK, :]
    mixed = totals.astype(BF16)
    inflow = jax.nn.sigmoid(
        jnp.dot(mixed, in_w[0], preferred_element_type=F32) + in_b[...]
    )
    recurrence = jax.nn.sigmoid(
        jnp.dot(mixed, de_w[0], preferred_element_type=F32) + de_b[...]
    )
    v = -param[...]
    soft = jnp.maximum(v, 0.0) + jnp.log1p(jnp.exp(-jnp.abs(v)))
    log_decay = recurrence * (-decay_power * soft)
    factor = jnp.exp(log_decay)
    push = (
        jnp.sqrt(negative_expm1(2.0 * log_decay, factor * factor))
        * inflow
        * mixed.astype(F32)
    )
    for lane in range(BLK // LANES):
        there = slice(lane * LANES, (lane + 1) * LANES)
        for r in range(SEGMENTS):
            rows = slice(r * STEPS, (r + 1) * STEPS)
            kept = slice(r * PITCH, r * PITCH + STEPS)
            factors[lane, kept, :] = factor[rows, there]
            pushes[lane, kept, :] = push[rows, there]

    lanes = range(BLK // LANES)
    product = [jnp.ones((SEGMENTS, LANES), F32) for _ in lanes]
    state = [jnp.zeros((SEGMENTS, LANES), F32) for _ in lanes]
    for t in range(STEPS):
        rows = pl.ds(t, SEGMENTS, stride=PITCH)
        for lane in lanes:
            f = factors[lane, rows, :]
            state[lane] = f * state[lane] + pushes[lane, rows, :]
            product[lane] = product[lane] * f
            pushes[lane, rows, :] = state[lane]
            factors[lane, rows, :] = product[lane]
    for lane in lanes:
        there = slice(lane * LANES, (lane + 1) * LANES)
        before_f = jnp.ones((1, LANES), F32)
        before_s = jnp.zeros((1, LANES), F32)
        for r in range(SEGMENTS):
            rows = slice(r * STEPS, (r + 1) * STEPS)
            g = gate[rows, there].astype(F32)
            g = 0.5 * g * (1.0 + jnp.tanh(0.7978845608028654 * (g + 0.044715 * (g * g * g))))
            kept = slice(r * PITCH, r * PITCH + STEPS)
            local_f = factors[lane, kept, :]
            u_out[rows, there] = (pushes[lane, kept, :] + local_f * before_s) * g
            w_out[rows, there] = (local_f * before_f) * g
            before_s = product[lane][r : r + 1] * before_s + state[lane][r : r + 1]
            before_f = product[lane][r : r + 1] * before_f
        end_out[0:1, there] = before_f
        end_out[1:2, there] = before_s


def recur(group, count, branch, edge, gate, taps, shift, in_w, in_b, de_w, de_b, param, filled):
    channels = branch.shape[1]
    lane = lambda rows: pl.BlockSpec((rows, BLK), lambda n: (0, n + group))
    square = pl.BlockSpec((1, BLK, BLK), lambda n: (n + group, 0, 0))
    kept = pl.BlockSpec(memory_space=pl.ANY)
    inputs = (branch, edge, gate, taps, shift, in_w, in_b, de_w, de_b, param)
    return pl.pallas_call(
        recur_kernel,
        name="recur",
        grid=(count,),
        out_shape=[
            jax.ShapeDtypeStruct((TOK, channels), F32),
            jax.ShapeDtypeStruct((TOK, channels), F32),
            jax.ShapeDtypeStruct((2, channels), F32),
        ],
        in_specs=[
            lane(TOK), lane(CONV - 1), lane(TOK), lane(CONV), lane(1),
            square, lane(1), square, lane(1), lane(1),
        ] + [kept] * len(filled),
        out_specs=[lane(TOK), lane(TOK), lane(2)],
        scratch_shapes=[
            pltpu.VMEM((TOK + 8, BLK), F32),
            pltpu.VMEM((BLK // LANES, SEGMENTS * PITCH, LANES), F32),
            pltpu.VMEM((BLK // LANES, SEGMENTS * PITCH, LANES), F32),
        ],
        input_output_aliases={len(inputs) + k: k for k in range(len(filled))},
        compiler_params=pltpu.CompilerParams(vmem_limit_bytes=ROOM),
        cost_estimate=pl.CostEstimate(
            flops=count << 28, bytes_accessed=count << 21, transcendentals=count << 20
        ),
    )(*inputs, *filled)


def attend_head(q_ref, kv, out, admitted):
    def scored(q, begin, size):
        return lax.dot_general(
            q,
            kv[begin : begin + size, 0:HD],
            (((1,), (1,)), ((), ())),
            preferred_element_type=F32,
        )

    rows = lax.broadcasted_iota(jnp.int32, (QROWS, QROWS), 0)
    columns = lax.broadcasted_iota(jnp.int32, (QROWS, QROWS), 1)
    causal = rows >= columns
    last = (SHARDS - 1) * TOK
    q = q_ref[...] * jnp.asarray(HD**-0.5, BF16)
    most = SHARDS - 1
    wide = [admitted(scored(q, k * TOK, TOK), most - k) for k in range(1, most)]
    for half in range(2):
        low = half * QROWS
        rows = slice(low, low + QROWS)
        far = admitted(scored(q[rows], low, QROWS), most)
        near = scored(q[rows], last + low, QROWS)
        blocks = [(k * TOK, s[rows]) for k, s in zip(range(1, SHARDS - 1), wide)]
        blocks.append((low, jnp.where(causal, masked_score, far)))
        blocks.append((last + low, jnp.where(causal, near, masked_score)))
        if half == 0:
            blocks.append((QROWS, admitted(scored(q[rows], QROWS, QROWS), most)))
        else:
            blocks.append((last, scored(q[rows], last, QROWS)))
        tiles = [s[:, k : k + 128] for _, s in blocks for k in range(0, s.shape[1], 128)]
        peak = jnp.max(functools.reduce(jnp.maximum, tiles), axis=1, keepdims=True)
        weights = [jnp.exp(s - peak) for _, s in blocks]
        tiles = [p[:, k : k + 128] for p in weights for k in range(0, p.shape[1], 128)]
        norm = jnp.sum(functools.reduce(jnp.add, tiles), axis=1, keepdims=True)
        total = jnp.zeros((QROWS, HD), F32)
        for p, (begin, _) in zip(weights, blocks):
            total = total + jnp.dot(
                p.astype(BF16),
                kv[begin : begin + p.shape[1], HD:],
                preferred_element_type=F32,
            )
        out[rows, :] = (total / norm).astype(BF16)


def attend_kernel(info, q_ref, *refs):
    own, other = (refs[0:PARTS], refs[PARTS : 2 * PARTS])
    out, kv = refs[-2:]
    core, position, place = (info[0], info[1], info[2])

    sources = (
        ((own, 0), (own, 2), (own, 1), (other, 1), (other, 2)),
        ((own, 0), (other, 0), (other, 2), (other, 1), (own, 1)),
    )
    for which in range(2):

        @pl.when((pl.program_id(0) == 0) & (core == which))
        def _():
            for k in range(PARTS):
                row = lax.rem(place + PARTS - k, PARTS) * QUARTER
                for behind, (pieces, slot) in enumerate(sources[which]):
                    there = (SHARDS - 1 - behind) * TOK + row
                    kv[pl.ds(pl.multiple_of(there, QUARTER), QUARTER), :] = pieces[k][
                        slot * QUARTER : (slot + 1) * QUARTER, :
                    ]

    @pl.when(position >= SHARDS - 1)
    def _():
        attend_head(q_ref, kv, out, lambda s, behind: s)

    @pl.when(position < SHARDS - 1)
    def _():
        attend_head(
            q_ref, kv, out, lambda s, behind: jnp.where(position >= behind, s, masked_score)
        )


def attend(head, count, info, queries, own, other, filled):
    block = pl.BlockSpec((TOK, HD), lambda h: (0, h + head))
    kept = pl.BlockSpec(memory_space=pl.ANY)
    inputs = (info, queries, *own, *other)
    return pl.pallas_call(
        attend_kernel,
        name="attend",
        grid=(count,),
        out_shape=jax.ShapeDtypeStruct(queries.shape, BF16),
        in_specs=[SMEM, block] + [whole(own[0].shape)] * (2 * PARTS) + [kept] * len(filled),
        out_specs=block,
        scratch_shapes=[pltpu.VMEM((SHARDS * TOK, 2 * HD), BF16)],
        input_output_aliases={len(inputs) + k: k for k in range(len(filled))},
        compiler_params=pltpu.CompilerParams(vmem_limit_bytes=32 << 20),
        cost_estimate=pl.CostEstimate(
            flops=count << 30, bytes_accessed=4 << 20, transcendentals=count << 20
        ),
    )(*inputs, *filled)


def shards(
    branch_in,
    branch_gate,
    conv_taps,
    conv_shift,
    inflow_weight,
    inflow_bias,
    decay_weight,
    decay_bias,
    decay_param,
    stream,
    norm_gain,
    memory_weight,
    queries,
):
    position = lax.axis_index(SEQ)
    core = lax.axis_index(CORE)
    turn = lax.axis_index("mp")
    place = turn.reshape(1)
    info = jnp.stack([core, position, turn]).astype(jnp.int32)
    line = lambda v: v.reshape(1, -1)

    edge = shifted(branch_in[TOK - (CONV - 1) :], 1)
    parts = project(place, stream, line(norm_gain), memory_weight)
    edge, *parts = lax.optimization_barrier((edge, *parts))
    arrived = [turned(parts[k], k) for k in range(1, PARTS)]
    rest = (
        branch_gate, conv_taps, line(conv_shift), inflow_weight, line(inflow_bias),
        decay_weight, line(decay_bias), line(decay_param),
    )
    groups = branch_in.shape[1] // BLK
    u, w, couple = recur(0, groups, branch_in, edge, *rest, ())
    own_part, couple = lax.optimization_barrier((parts[0], couple))
    mine = normed([own_part] + arrived, couple)
    pair = jnp.concatenate([mine, swapped(mine)])
    trio, before, inclusive, got = window(info, pair, forked(pair, 1, 2), branch_in.shape[1])
    own = [trio] + [turned(trio, k) for k in range(1, PARTS)]
    before, inclusive = merged(info, before, inclusive, got, swapped(got))
    far = [forked(inclusive, 3, 6), forked(inclusive, 9, 12)]
    *far, own[1], own[2], own[3] = lax.optimization_barrier((*far, *own[1:]))
    far = jnp.concatenate(far)
    before, inclusive = merged(info, before, inclusive, far, swapped(far))
    other = [swapped(piece) for piece in own]
    far = forked(inclusive, 15, 30)
    heads = queries.shape[1] // HD
    attended = attend(0, heads, info, queries, own, other, ())
    far, attended = lax.optimization_barrier((far, attended))
    before, _ = merged(info, before, inclusive, far, swapped(far))
    recurrent_out = (u + w * before[1:2]).astype(BF16)
    return (recurrent_out, attended)


def solution(mesh):
    finer = Mesh(mesh.devices.reshape(8, 4, 2, mesh.shape["mp"]), (*SEQ, "mp"))
    in_specs = (
        P(SEQ, "mp"),
        P(SEQ, "mp"),
        P(None, "mp"),
        P("mp"),
        P("mp", None, None),
        P("mp"),
        P("mp", None, None),
        P("mp"),
        P("mp"),
        P(SEQ, "mp"),
        P("mp"),
        P("mp", None),
        P(SEQ, "mp"),
    )
    out_specs = (P(SEQ, "mp"), P(SEQ, "mp"))
    return jax.shard_map(
        shards, mesh=finer, in_specs=in_specs, out_specs=out_specs, check_vma=False
    )
```

```python
import functools

import jax
import jax.numpy as jnp
from jax import lax
from jax.experimental import pallas as pl
from jax.experimental.pallas import tpu as pltpu
from jax.sharding import Mesh
from jax.sharding import PartitionSpec as P

D = 4096
HD = 256
CONV = 4
WINDOW = 2048
BLK = 256
SEQ = ("seq_0", "seq_1", "seq_2")
CORE = "seq_2"
TOK = 512
QUARTER = 128
PARTS = 4
SEGMENTS = 8
STEPS = TOK // SEGMENTS
PITCH = STEPS + 1
QROWS = 256
LANES = 128
EXTRA = 16
ROOM = 60 << 20
SHARDS = 5

decay_power = 8.0
norm_epsilon = 1e-06
masked_score = -1e30
F32 = jnp.float32
BF16 = jnp.bfloat16
SMEM = pl.BlockSpec(memory_space=pltpu.SMEM)


def whole(shape):
    return pl.BlockSpec(shape, lambda *_: (0,) * len(shape))


def shifted(value, steps):
    count = lax.axis_size(SEQ)
    return lax.ppermute(value, SEQ, [(k, k + steps) for k in range(count - steps)])


def forked(value, near, distant):
    chips = lax.axis_size(SEQ) // 2
    pairs = [(2 * c, 2 * (c + near)) for c in range(chips - near)]
    pairs += [(2 * c + 1, 2 * (c + distant) + 1) for c in range(chips - distant)]
    return lax.ppermute(value, SEQ, pairs)


def turned(value, steps):
    return lax.ppermute(value, "mp", [(k, (k + steps) % PARTS) for k in range(PARTS)])


def swapped(value):
    return lax.ppermute(value, CORE, [(0, 1), (1, 0)])


def project_kernel(place, stream, gain, weight, *parts):
    row = lax.broadcasted_iota(jnp.int32, (EXTRA, QUARTER), 0)
    for k, part in enumerate(parts):
        start = pl.multiple_of(lax.rem(place[0] + k, PARTS) * QUARTER, QUARTER)
        x = stream[pl.ds(start, QUARTER), :].astype(F32)
        squares = jnp.sum(x * x, axis=1, keepdims=True)
        scaled = (x * gain[...]).astype(BF16)
        product = jnp.dot(scaled, weight[...], preferred_element_type=F32)
        part[0:QUARTER, :] = product.astype(part.dtype)
        part[QUARTER:, :] = jnp.zeros((EXTRA, 2 * HD), part.dtype)
        line = jnp.broadcast_to(squares, (QUARTER, QUARTER)).T[0:EXTRA]
        high = line.astype(BF16).astype(F32)
        line = jnp.where(row == 0, high, jnp.where(row == 1, line - high, 0.0))
        part[QUARTER:, 0:QUARTER] = line.astype(part.dtype)


def project(place, stream, gain, weight):
    shape = (QUARTER + EXTRA, 2 * HD)
    return pl.pallas_call(
        project_kernel,
        name="project",
        out_shape=[jax.ShapeDtypeStruct(shape, F32 if k == 0 else BF16) for k in range(PARTS)],
        in_specs=[SMEM, whole(stream.shape), whole(gain.shape), whole(weight.shape)],
        out_specs=[whole(shape)] * PARTS,
        compiler_params=pltpu.CompilerParams(vmem_limit_bytes=ROOM),
        cost_estimate=pl.CostEstimate(flops=1 << 29, bytes_accessed=3 << 20, transcendentals=0),
    )(place, stream, gain, weight)


def split(value):
    high = value.astype(BF16).astype(F32)
    rest = value - high
    middle = rest.astype(BF16).astype(F32)
    return (high, middle, rest - middle)


def norm_kernel(a, b, c, d, couple, out):
    total = (a[...] + b[...].astype(F32)) + (c[...].astype(F32) + d[...].astype(F32))
    line = total[QUARTER : QUARTER + 1, 0:QUARTER] + total[QUARTER + 1 : QUARTER + 2, 0:QUARTER]
    column = jnp.broadcast_to(line, (QUARTER, QUARTER)).T[:, 0:1]
    root = jnp.sqrt(column / D + norm_epsilon)
    out[0:QUARTER, :] = (total[0:QUARTER] / root).astype(BF16)
    width = 2 * HD
    lines = [
        part[:, k : k + width]
        for value in (couple[0:1, :], couple[1:2, :])
        for part in split(value)
        for k in range(0, value.shape[1], width)
    ]
    lines += [jnp.zeros((1, width), F32)] * (EXTRA - len(lines))
    out[QUARTER:, :] = jnp.concatenate(lines).astype(BF16)


def normed(parts, couple):
    shape = parts[0].shape
    return pl.pallas_call(
        norm_kernel,
        name="normed",
        out_shape=jax.ShapeDtypeStruct(shape, BF16),
        in_specs=[whole(shape)] * PARTS + [whole(couple.shape)],
        out_specs=whole(shape),
        compiler_params=pltpu.CompilerParams(vmem_limit_bytes=8 << 20),
        cost_estimate=pl.CostEstimate(flops=1 << 20, bytes_accessed=5 << 17, transcendentals=0),
    )(*parts, couple)


def received(lines, channels):
    values = []
    width = 2 * HD
    per = channels // width
    for value in range(2):
        halves = []
        for k in range(per):
            at = [value * 3 * per + part * per + k for part in range(3)]
            high, middle, low = [lines[row : row + 1] for row in at]
            halves.append(high + (middle + low))
        values.append(jnp.concatenate(halves, axis=1))
    return values


def applied(earlier, later):
    return (earlier[0] * later[0], later[0] * earlier[1] + later[1])


def chosen(flag, first, second):
    return [jnp.where(flag, x, y) for x, y in zip(first, second)]


def window_kernel(info, pair, arrived, duo, before, inclusive, got):
    channels = before.shape[1]
    first = info[0] == 0
    each = QUARTER + EXTRA
    duo[0:QUARTER, :] = arrived[0:QUARTER, :]
    duo[QUARTER:, :] = arrived[each : each + QUARTER, :]
    for ref, out in ((pair, inclusive), (arrived, got)):
        mine = received(ref[QUARTER:each, :].astype(F32), channels)
        theirs = received(ref[each + QUARTER :, :].astype(F32), channels)
        chip = applied(chosen(first, mine, theirs), chosen(first, theirs, mine))
        out[0:1, :], out[1:2, :] = chip
        if ref is pair:
            none = (jnp.ones_like(theirs[0]), jnp.zeros_like(theirs[1]))
            before[0:1, :], before[1:2, :] = chosen(first, none, theirs)


def window(info, pair, arrived, channels):
    shape = (2 * QUARTER, 2 * HD)
    couple = (2, channels)
    return pl.pallas_call(
        window_kernel,
        name="window",
        out_shape=[jax.ShapeDtypeStruct(shape, BF16)] + [jax.ShapeDtypeStruct(couple, F32)] * 3,
        in_specs=[SMEM] + [whole(pair.shape)] * 2,
        out_specs=[whole(shape)] + [whole(couple)] * 3,
        compiler_params=pltpu.CompilerParams(vmem_limit_bytes=8 << 20),
        cost_estimate=pl.CostEstimate(flops=1 << 14, bytes_accessed=3 << 18, transcendentals=0),
    )(info, pair, arrived)


def merge_kernel(info, before, inclusive, mine, theirs, before_out, inclusive_out):
    first = info[0] == 0
    passed = (before[0:1, :], before[1:2, :])
    covered = (inclusive[0:1, :], inclusive[1:2, :])
    for at in range(0, mine.shape[0], 2):
        ours = (mine[at : at + 1, :], mine[at + 1 : at + 2, :])
        other = (theirs[at : at + 1, :], theirs[at + 1 : at + 2, :])
        for earlier in (chosen(first, ours, other), chosen(first, other, ours)):
            passed = applied(earlier, passed)
            covered = applied(earlier, covered)
    before_out[0:1, :], before_out[1:2, :] = passed
    inclusive_out[0:1, :], inclusive_out[1:2, :] = covered


def merged(info, before, inclusive, mine, theirs):
    couple = whole(before.shape)
    return pl.pallas_call(
        merge_kernel,
        name="merged",
        out_shape=[jax.ShapeDtypeStruct(before.shape, F32)] * 2,
        in_specs=[SMEM, couple, couple, whole(mine.shape), whole(mine.shape)],
        out_specs=[couple, couple],
        compiler_params=pltpu.CompilerParams(vmem_limit_bytes=4 << 20),
        cost_estimate=pl.CostEstimate(flops=1 << 14, bytes_accessed=1 << 16, transcendentals=0),
    )(info, before, inclusive, mine, theirs)


def negative_expm1(y, grown):
    series = jnp.full_like(y, 1.0)
    for k in (8, 7, 6, 5, 4, 3, 2):
        series = 1.0 + series * (y * (1.0 / k))
    return jnp.where(y > -0.5, -y * series, 1.0 - grown)


def recur_kernel(
    branch, edge, gate, taps, shift, in_w, in_b, de_w, de_b, param, *rest
):
    u_out, w_out, end_out, extended, factors, pushes = rest[-6:]
    extended[8 : 8 + TOK, :] = branch[...].astype(F32)
    extended[8 - (CONV - 1) : 8, :] = edge[...].astype(F32)
    totals = shift[...] + taps[0:1, :] * extended[8 : 8 + TOK, :]
    for k in range(1, CONV):
        totals = totals + taps[k : k + 1, :] * extended[8 - k : 8 - k + TOK, :]
    mixed = totals.astype(BF16)
    inflow = jax.nn.sigmoid(
        jnp.dot(mixed, in_w[0], preferred_element_type=F32) + in_b[...]
    )
    recurrence = jax.nn.sigmoid(
        jnp.dot(mixed, de_w[0], preferred_element_type=F32) + de_b[...]
    )
    v = -param[...]
    soft = jnp.maximum(v, 0.0) + jnp.log1p(jnp.exp(-jnp.abs(v)))
    log_decay = recurrence * (-decay_power * soft)
    factor = jnp.exp(log_decay)
    push = (
        jnp.sqrt(negative_expm1(2.0 * log_decay, factor * factor))
        * inflow
        * mixed.astype(F32)
    )
    for lane in range(BLK // LANES):
        there = slice(lane * LANES, (lane + 1) * LANES)
        for r in range(SEGMENTS):
            rows = slice(r * STEPS, (r + 1) * STEPS)
            kept = slice(r * PITCH, r * PITCH + STEPS)
            factors[lane, kept, :] = factor[rows, there]
            pushes[lane, kept, :] = push[rows, there]

    lanes = range(BLK // LANES)
    product = [jnp.ones((SEGMENTS, LANES), F32) for _ in lanes]
    state = [jnp.zeros((SEGMENTS, LANES), F32) for _ in lanes]
    for t in range(STEPS):
        rows = pl.ds(t, SEGMENTS, stride=PITCH)
        for lane in lanes:
            f = factors[lane, rows, :]
            state[lane] = f * state[lane] + pushes[lane, rows, :]
            product[lane] = product[lane] * f
            pushes[lane, rows, :] = state[lane]
            factors[lane, rows, :] = product[lane]
    for lane in lanes:
        there = slice(lane * LANES, (lane + 1) * LANES)
        before_f = jnp.ones((1, LANES), F32)
        before_s = jnp.zeros((1, LANES), F32)
        for r in range(SEGMENTS):
            rows = slice(r * STEPS, (r + 1) * STEPS)
            g = gate[rows, there].astype(F32)
            g = 0.5 * g * (1.0 + jnp.tanh(0.7978845608028654 * (g + 0.044715 * (g * g * g))))
            kept = slice(r * PITCH, r * PITCH + STEPS)
            local_f = factors[lane, kept, :]
            u_out[rows, there] = (pushes[lane, kept, :] + local_f * before_s) * g
            w_out[rows, there] = (local_f * before_f) * g
            before_s = product[lane][r : r + 1] * before_s + state[lane][r : r + 1]
            before_f = product[lane][r : r + 1] * before_f
        end_out[0:1, there] = before_f
        end_out[1:2, there] = before_s


def recur(group, count, branch, edge, gate, taps, shift, in_w, in_b, de_w, de_b, param, filled):
    channels = branch.shape[1]
    lane = lambda rows: pl.BlockSpec((rows, BLK), lambda n: (0, n + group))
    square = pl.BlockSpec((1, BLK, BLK), lambda n: (n + group, 0, 0))
    kept = pl.BlockSpec(memory_space=pl.ANY)
    inputs = (branch, edge, gate, taps, shift, in_w, in_b, de_w, de_b, param)
    return pl.pallas_call(
        recur_kernel,
        name="recur",
        grid=(count,),
        out_shape=[
            jax.ShapeDtypeStruct((TOK, channels), F32),
            jax.ShapeDtypeStruct((TOK, channels), F32),
            jax.ShapeDtypeStruct((2, channels), F32),
        ],
        in_specs=[
            lane(TOK), lane(CONV - 1), lane(TOK), lane(CONV), lane(1),
            square, lane(1), square, lane(1), lane(1),
        ] + [kept] * len(filled),
        out_specs=[lane(TOK), lane(TOK), lane(2)],
        scratch_shapes=[
            pltpu.VMEM((TOK + 8, BLK), F32),
            pltpu.VMEM((BLK // LANES, SEGMENTS * PITCH, LANES), F32),
            pltpu.VMEM((BLK // LANES, SEGMENTS * PITCH, LANES), F32),
        ],
        input_output_aliases={len(inputs) + k: k for k in range(len(filled))},
        compiler_params=pltpu.CompilerParams(vmem_limit_bytes=ROOM),
        cost_estimate=pl.CostEstimate(
            flops=count << 28, bytes_accessed=count << 21, transcendentals=count << 20
        ),
    )(*inputs, *filled)


def attend_head(q_ref, kv, out, admitted):
    def scored(q, begin, size):
        return lax.dot_general(
            q,
            kv[begin : begin + size, 0:HD],
            (((1,), (1,)), ((), ())),
            preferred_element_type=F32,
        )

    rows = lax.broadcasted_iota(jnp.int32, (QROWS, QROWS), 0)
    columns = lax.broadcasted_iota(jnp.int32, (QROWS, QROWS), 1)
    causal = rows >= columns
    last = (SHARDS - 1) * TOK
    q = q_ref[...] * jnp.asarray(HD**-0.5, BF16)
    most = SHARDS - 1
    wide = [admitted(scored(q, k * TOK, TOK), most - k) for k in range(1, most)]
    for half in range(2):
        low = half * QROWS
        rows = slice(low, low + QROWS)
        far = admitted(scored(q[rows], low, QROWS), most)
        near = scored(q[rows], last + low, QROWS)
        blocks = [(k * TOK, s[rows]) for k, s in zip(range(1, SHARDS - 1), wide)]
        blocks.append((low, jnp.where(causal, masked_score, far)))
        blocks.append((last + low, jnp.where(causal, near, masked_score)))
        if half == 0:
            blocks.append((QROWS, admitted(scored(q[rows], QROWS, QROWS), most)))
        else:
            blocks.append((last, scored(q[rows], last, QROWS)))
        tiles = [s[:, k : k + 128] for _, s in blocks for k in range(0, s.shape[1], 128)]
        peak = jnp.max(functools.reduce(jnp.maximum, tiles), axis=1, keepdims=True)
        weights = [jnp.exp(s - peak) for _, s in blocks]
        tiles = [p[:, k : k + 128] for p in weights for k in range(0, p.shape[1], 128)]
        norm = jnp.sum(functools.reduce(jnp.add, tiles), axis=1, keepdims=True)
        total = jnp.zeros((QROWS, HD), F32)
        for p, (begin, _) in zip(weights, blocks):
            total = total + jnp.dot(
                p.astype(BF16),
                kv[begin : begin + p.shape[1], HD:],
                preferred_element_type=F32,
            )
        out[rows, :] = (total / norm).astype(BF16)


def attend_kernel(info, q_ref, *refs):
    own, two, other, others = [refs[k * PARTS : (k + 1) * PARTS] for k in range(4)]
    out, kv = refs[-2:]
    core, position, place = (info[0], info[1], info[2])

    sources = (
        ((own, 0), (two, 1), (two, 0), (others, 0), (others, 1)),
        ((own, 0), (other, 0), (others, 1), (others, 0), (two, 0)),
    )
    for which in range(2):

        @pl.when((pl.program_id(0) == 0) & (core == which))
        def _():
            for k in range(PARTS):
                row = lax.rem(place + PARTS - k, PARTS) * QUARTER
                for behind, (pieces, slot) in enumerate(sources[which]):
                    there = (SHARDS - 1 - behind) * TOK + row
                    kv[pl.ds(pl.multiple_of(there, QUARTER), QUARTER), :] = pieces[k][
                        slot * QUARTER : (slot + 1) * QUARTER, :
                    ]

    @pl.when(position >= SHARDS - 1)
    def _():
        attend_head(q_ref, kv, out, lambda s, behind: s)

    @pl.when(position < SHARDS - 1)
    def _():
        attend_head(
            q_ref, kv, out, lambda s, behind: jnp.where(position >= behind, s, masked_score)
        )


def attend(head, count, info, queries, pieces, filled):
    block = pl.BlockSpec((TOK, HD), lambda h: (0, h + head))
    kept = pl.BlockSpec(memory_space=pl.ANY)
    inputs = (info, queries, *pieces)
    return pl.pallas_call(
        attend_kernel,
        name="attend",
        grid=(count,),
        out_shape=jax.ShapeDtypeStruct(queries.shape, BF16),
        in_specs=[SMEM, block] + [whole(piece.shape) for piece in pieces] + [kept] * len(filled),
        out_specs=block,
        scratch_shapes=[pltpu.VMEM((SHARDS * TOK, 2 * HD), BF16)],
        input_output_aliases={len(inputs) + k: k for k in range(len(filled))},
        compiler_params=pltpu.CompilerParams(vmem_limit_bytes=32 << 20),
        cost_estimate=pl.CostEstimate(
            flops=count << 30, bytes_accessed=4 << 20, transcendentals=count << 20
        ),
    )(*inputs, *filled)


def shards(
    branch_in,
    branch_gate,
    conv_taps,
    conv_shift,
    inflow_weight,
    inflow_bias,
    decay_weight,
    decay_bias,
    decay_param,
    stream,
    norm_gain,
    memory_weight,
    queries,
):
    position = lax.axis_index(SEQ)
    core = lax.axis_index(CORE)
    turn = lax.axis_index("mp")
    place = turn.reshape(1)
    info = jnp.stack([core, position, turn]).astype(jnp.int32)
    line = lambda v: v.reshape(1, -1)

    edge = shifted(branch_in[TOK - (CONV - 1) :], 1)
    parts = project(place, stream, line(norm_gain), memory_weight)
    edge, *parts = lax.optimization_barrier((edge, *parts))
    arrived = [turned(parts[k], k) for k in range(1, PARTS)]
    rest = (
        branch_gate, conv_taps, line(conv_shift), inflow_weight, line(inflow_bias),
        decay_weight, line(decay_bias), line(decay_param),
    )
    groups = branch_in.shape[1] // BLK
    u, w, couple = recur(0, groups, branch_in, edge, *rest, ())
    own_part, couple = lax.optimization_barrier((parts[0], couple))
    mine = normed([own_part] + arrived, couple)
    beside = swapped(mine)
    pair = jnp.concatenate([mine, beside])
    own = [turned(mine, k) for k in range(1, PARTS)]
    arrived, *own = lax.optimization_barrier((forked(pair, 1, 2), *own))
    duo, before, inclusive, got = window(info, pair, arrived, branch_in.shape[1])
    two = [turned(duo, k) for k in range(1, PARTS)]
    before, inclusive = merged(info, before, inclusive, got, swapped(got))
    far = [forked(inclusive, 3, 6), forked(inclusive, 9, 12)]
    far, two, own, duo = lax.optimization_barrier((far, two, own, duo))
    other = [swapped(piece) for piece in own]
    far = jnp.concatenate(far)
    before, inclusive = merged(info, before, inclusive, far, swapped(far))
    two = [duo] + two
    others = [swapped(piece) for piece in two]
    far = [shifted(inclusive, 30), shifted(inclusive, 60)]
    heads = queries.shape[1] // HD
    pieces = (mine, *own, *two, beside, *other, *others)
    attended = attend(0, heads, info, queries, pieces, ())
    *far, attended = lax.optimization_barrier((*far, attended))
    state = far[0][0:1] * far[1][1:2] + far[0][1:2]
    state = before[0:1] * state + before[1:2]
    recurrent_out = (u + w * state).astype(BF16)
    return (recurrent_out, attended)


def solution(mesh):
    finer = Mesh(mesh.devices.reshape(8, 4, 2, mesh.shape["mp"]), (*SEQ, "mp"))
    in_specs = (
        P(SEQ, "mp"),
        P(SEQ, "mp"),
        P(None, "mp"),
        P("mp"),
        P("mp", None, None),
        P("mp"),
        P("mp", None, None),
        P("mp"),
        P("mp"),
        P(SEQ, "mp"),
        P("mp"),
        P("mp", None),
        P(SEQ, "mp"),
    )
    out_specs = (P(SEQ, "mp"), P(SEQ, "mp"))
    return jax.shard_map(
        shards, mesh=finer, in_specs=in_specs, out_specs=out_specs, check_vma=False
    )
```

```python
import functools

import jax
import jax.numpy as jnp
from jax import lax
from jax.experimental import pallas as pl
from jax.experimental.pallas import tpu as pltpu
from jax.sharding import Mesh
from jax.sharding import PartitionSpec as P

D = 4096
HD = 256
CONV = 4
WINDOW = 2048
BLK = 256
SEQ = ("seq_0", "seq_1", "seq_2")
CORE = "seq_2"
TOK = 512
QUARTER = 128
PARTS = 4
SEGMENTS = 8
STEPS = TOK // SEGMENTS
PITCH = STEPS + 1
QROWS = 256
LANES = 128
EXTRA = 16
ROOM = 60 << 20
SHARDS = 5

decay_power = 8.0
norm_epsilon = 1e-06
masked_score = -1e30
F32 = jnp.float32
BF16 = jnp.bfloat16
SMEM = pl.BlockSpec(memory_space=pltpu.SMEM)


def whole(shape):
    return pl.BlockSpec(shape, lambda *_: (0,) * len(shape))


def shifted(value, steps):
    count = lax.axis_size(SEQ)
    return lax.ppermute(value, SEQ, [(k, k + steps) for k in range(count - steps)])


def forked(value, near, distant):
    chips = lax.axis_size(SEQ) // 2
    pairs = [(2 * c, 2 * (c + near)) for c in range(chips - near)]
    pairs += [(2 * c + 1, 2 * (c + distant) + 1) for c in range(chips - distant)]
    return lax.ppermute(value, SEQ, pairs)


def turned(value, steps):
    return lax.ppermute(value, "mp", [(k, (k + steps) % PARTS) for k in range(PARTS)])


def swapped(value):
    return lax.ppermute(value, CORE, [(0, 1), (1, 0)])


def project_kernel(place, stream, gain, weight, *parts):
    row = lax.broadcasted_iota(jnp.int32, (EXTRA, QUARTER), 0)
    for k, part in enumerate(parts):
        start = pl.multiple_of(lax.rem(place[0] + k, PARTS) * QUARTER, QUARTER)
        x = stream[pl.ds(start, QUARTER), :].astype(F32)
        squares = jnp.sum(x * x, axis=1, keepdims=True)
        scaled = (x * gain[...]).astype(BF16)
        product = jnp.dot(scaled, weight[...], preferred_element_type=F32)
        part[0:QUARTER, :] = product.astype(part.dtype)
        part[QUARTER:, :] = jnp.zeros((EXTRA, 2 * HD), part.dtype)
        line = jnp.broadcast_to(squares, (QUARTER, QUARTER)).T[0:EXTRA]
        high = line.astype(BF16).astype(F32)
        line = jnp.where(row == 0, high, jnp.where(row == 1, line - high, 0.0))
        part[QUARTER:, 0:QUARTER] = line.astype(part.dtype)


def project(place, stream, gain, weight):
    shape = (QUARTER + EXTRA, 2 * HD)
    return pl.pallas_call(
        project_kernel,
        name="project",
        out_shape=[jax.ShapeDtypeStruct(shape, F32 if k == 0 else BF16) for k in range(PARTS)],
        in_specs=[SMEM, whole(stream.shape), whole(gain.shape), whole(weight.shape)],
        out_specs=[whole(shape)] * PARTS,
        compiler_params=pltpu.CompilerParams(vmem_limit_bytes=ROOM),
        cost_estimate=pl.CostEstimate(flops=1 << 29, bytes_accessed=3 << 20, transcendentals=0),
    )(place, stream, gain, weight)


def split(value):
    high = value.astype(BF16).astype(F32)
    rest = value - high
    middle = rest.astype(BF16).astype(F32)
    return (high, middle, rest - middle)


def norm_kernel(a, b, c, d, couple, out):
    total = (a[...] + b[...].astype(F32)) + (c[...].astype(F32) + d[...].astype(F32))
    line = total[QUARTER : QUARTER + 1, 0:QUARTER] + total[QUARTER + 1 : QUARTER + 2, 0:QUARTER]
    column = jnp.broadcast_to(line, (QUARTER, QUARTER)).T[:, 0:1]
    root = jnp.sqrt(column / D + norm_epsilon)
    out[0:QUARTER, :] = (total[0:QUARTER] / root).astype(BF16)
    width = 2 * HD
    lines = [
        part[:, k : k + width]
        for value in (couple[0:1, :], couple[1:2, :])
        for part in split(value)
        for k in range(0, value.shape[1], width)
    ]
    lines += [jnp.zeros((1, width), F32)] * (EXTRA - len(lines))
    out[QUARTER:, :] = jnp.concatenate(lines).astype(BF16)


def normed(parts, couple):
    shape = parts[0].shape
    return pl.pallas_call(
        norm_kernel,
        name="normed",
        out_shape=jax.ShapeDtypeStruct(shape, BF16),
        in_specs=[whole(shape)] * PARTS + [whole(couple.shape)],
        out_specs=whole(shape),
        compiler_params=pltpu.CompilerParams(vmem_limit_bytes=8 << 20),
        cost_estimate=pl.CostEstimate(flops=1 << 20, bytes_accessed=5 << 17, transcendentals=0),
    )(*parts, couple)


def received(lines, channels):
    values = []
    width = 2 * HD
    per = channels // width
    for value in range(2):
        halves = []
        for k in range(per):
            at = [value * 3 * per + part * per + k for part in range(3)]
            high, middle, low = [lines[row : row + 1] for row in at]
            halves.append(high + (middle + low))
        values.append(jnp.concatenate(halves, axis=1))
    return values


def applied(earlier, later):
    return (earlier[0] * later[0], later[0] * earlier[1] + later[1])


def chosen(flag, first, second):
    return [jnp.where(flag, x, y) for x, y in zip(first, second)]


def window_kernel(info, pair, arrived, duo, before, inclusive, got):
    channels = before.shape[1]
    first = info[0] == 0
    each = QUARTER + EXTRA
    duo[0:QUARTER, :] = arrived[0:QUARTER, :]
    duo[QUARTER:, :] = arrived[each : each + QUARTER, :]
    for ref, out in ((pair, inclusive), (arrived, got)):
        mine = received(ref[QUARTER:each, :].astype(F32), channels)
        theirs = received(ref[each + QUARTER :, :].astype(F32), channels)
        chip = applied(chosen(first, mine, theirs), chosen(first, theirs, mine))
        out[0:1, :], out[1:2, :] = chip
        if ref is pair:
            none = (jnp.ones_like(theirs[0]), jnp.zeros_like(theirs[1]))
            before[0:1, :], before[1:2, :] = chosen(first, none, theirs)


def window(info, pair, arrived, channels):
    shape = (2 * QUARTER, 2 * HD)
    couple = (2, channels)
    return pl.pallas_call(
        window_kernel,
        name="window",
        out_shape=[jax.ShapeDtypeStruct(shape, BF16)] + [jax.ShapeDtypeStruct(couple, F32)] * 3,
        in_specs=[SMEM] + [whole(pair.shape)] * 2,
        out_specs=[whole(shape)] + [whole(couple)] * 3,
        compiler_params=pltpu.CompilerParams(vmem_limit_bytes=8 << 20),
        cost_estimate=pl.CostEstimate(flops=1 << 14, bytes_accessed=3 << 18, transcendentals=0),
    )(info, pair, arrived)


def merge_kernel(info, before, inclusive, mine, theirs, before_out, inclusive_out):
    first = info[0] == 0
    passed = (before[0:1, :], before[1:2, :])
    covered = (inclusive[0:1, :], inclusive[1:2, :])
    for at in range(0, mine.shape[0], 2):
        ours = (mine[at : at + 1, :], mine[at + 1 : at + 2, :])
        other = (theirs[at : at + 1, :], theirs[at + 1 : at + 2, :])
        for earlier in (chosen(first, ours, other), chosen(first, other, ours)):
            passed = applied(earlier, passed)
            covered = applied(earlier, covered)
    before_out[0:1, :], before_out[1:2, :] = passed
    inclusive_out[0:1, :], inclusive_out[1:2, :] = covered


def merged(info, before, inclusive, mine, theirs):
    couple = whole(before.shape)
    return pl.pallas_call(
        merge_kernel,
        name="merged",
        out_shape=[jax.ShapeDtypeStruct(before.shape, F32)] * 2,
        in_specs=[SMEM, couple, couple, whole(mine.shape), whole(mine.shape)],
        out_specs=[couple, couple],
        compiler_params=pltpu.CompilerParams(vmem_limit_bytes=4 << 20),
        cost_estimate=pl.CostEstimate(flops=1 << 14, bytes_accessed=1 << 16, transcendentals=0),
    )(info, before, inclusive, mine, theirs)


def negative_expm1(y, grown):
    series = jnp.full_like(y, 1.0)
    for k in (8, 7, 6, 5, 4, 3, 2):
        series = 1.0 + series * (y * (1.0 / k))
    return jnp.where(y > -0.5, -y * series, 1.0 - grown)


def recur_kernel(
    branch, edge, gate, taps, shift, in_w, in_b, de_w, de_b, param, *rest
):
    u_out, w_out, end_out, extended, factors, pushes = rest[-6:]
    extended[8 : 8 + TOK, :] = branch[...].astype(F32)
    extended[8 - (CONV - 1) : 8, :] = edge[...].astype(F32)
    totals = shift[...] + taps[0:1, :] * extended[8 : 8 + TOK, :]
    for k in range(1, CONV):
        totals = totals + taps[k : k + 1, :] * extended[8 - k : 8 - k + TOK, :]
    mixed = totals.astype(BF16)
    inflow = jax.nn.sigmoid(
        jnp.dot(mixed, in_w[0], preferred_element_type=F32) + in_b[...]
    )
    recurrence = jax.nn.sigmoid(
        jnp.dot(mixed, de_w[0], preferred_element_type=F32) + de_b[...]
    )
    v = -param[...]
    soft = jnp.maximum(v, 0.0) + jnp.log1p(jnp.exp(-jnp.abs(v)))
    log_decay = recurrence * (-decay_power * soft)
    factor = jnp.exp(log_decay)
    push = (
        jnp.sqrt(negative_expm1(2.0 * log_decay, factor * factor))
        * inflow
        * mixed.astype(F32)
    )
    for lane in range(BLK // LANES):
        there = slice(lane * LANES, (lane + 1) * LANES)
        for r in range(SEGMENTS):
            rows = slice(r * STEPS, (r + 1) * STEPS)
            kept = slice(r * PITCH, r * PITCH + STEPS)
            factors[lane, kept, :] = factor[rows, there]
            pushes[lane, kept, :] = push[rows, there]

    lanes = range(BLK // LANES)
    product = [jnp.ones((SEGMENTS, LANES), F32) for _ in lanes]
    state = [jnp.zeros((SEGMENTS, LANES), F32) for _ in lanes]
    for t in range(STEPS):
        rows = pl.ds(t, SEGMENTS, stride=PITCH)
        for lane in lanes:
            f = factors[lane, rows, :]
            state[lane] = f * state[lane] + pushes[lane, rows, :]
            product[lane] = product[lane] * f
            pushes[lane, rows, :] = state[lane]
            factors[lane, rows, :] = product[lane]
    for lane in lanes:
        there = slice(lane * LANES, (lane + 1) * LANES)
        before_f = jnp.ones((1, LANES), F32)
        before_s = jnp.zeros((1, LANES), F32)
        for r in range(SEGMENTS):
            rows = slice(r * STEPS, (r + 1) * STEPS)
            g = gate[rows, there].astype(F32)
            g = 0.5 * g * (1.0 + jnp.tanh(0.7978845608028654 * (g + 0.044715 * (g * g * g))))
            kept = slice(r * PITCH, r * PITCH + STEPS)
            local_f = factors[lane, kept, :]
            u_out[rows, there] = (pushes[lane, kept, :] + local_f * before_s) * g
            w_out[rows, there] = (local_f * before_f) * g
            before_s = product[lane][r : r + 1] * before_s + state[lane][r : r + 1]
            before_f = product[lane][r : r + 1] * before_f
        end_out[0:1, there] = before_f
        end_out[1:2, there] = before_s


def recur(group, count, branch, edge, gate, taps, shift, in_w, in_b, de_w, de_b, param, filled):
    channels = branch.shape[1]
    lane = lambda rows: pl.BlockSpec((rows, BLK), lambda n: (0, n + group))
    square = pl.BlockSpec((1, BLK, BLK), lambda n: (n + group, 0, 0))
    kept = pl.BlockSpec(memory_space=pl.ANY)
    inputs = (branch, edge, gate, taps, shift, in_w, in_b, de_w, de_b, param)
    return pl.pallas_call(
        recur_kernel,
        name="recur",
        grid=(count,),
        out_shape=[
            jax.ShapeDtypeStruct((TOK, channels), F32),
            jax.ShapeDtypeStruct((TOK, channels), F32),
            jax.ShapeDtypeStruct((2, channels), F32),
        ],
        in_specs=[
            lane(TOK), lane(CONV - 1), lane(TOK), lane(CONV), lane(1),
            square, lane(1), square, lane(1), lane(1),
        ] + [kept] * len(filled),
        out_specs=[lane(TOK), lane(TOK), lane(2)],
        scratch_shapes=[
            pltpu.VMEM((TOK + 8, BLK), F32),
            pltpu.VMEM((BLK // LANES, SEGMENTS * PITCH, LANES), F32),
            pltpu.VMEM((BLK // LANES, SEGMENTS * PITCH, LANES), F32),
        ],
        input_output_aliases={len(inputs) + k: k for k in range(len(filled))},
        compiler_params=pltpu.CompilerParams(vmem_limit_bytes=ROOM),
        cost_estimate=pl.CostEstimate(
            flops=count << 28, bytes_accessed=count << 21, transcendentals=count << 20
        ),
    )(*inputs, *filled)


def attend_head(q_ref, kv, out, earlier):
    def scored(q, begin, size):
        return lax.dot_general(
            q,
            kv[begin : begin + size, 0:HD],
            (((1,), (1,)), ((), ())),
            preferred_element_type=F32,
        )

    rows = lax.broadcasted_iota(jnp.int32, (QROWS, QROWS), 0)
    columns = lax.broadcasted_iota(jnp.int32, (QROWS, QROWS), 1)
    causal = rows >= columns
    last = (SHARDS - 1) * TOK
    q = q_ref[...] * jnp.asarray(HD**-0.5, BF16)
    most = SHARDS - 1
    whole_shards = range(max(1, most - earlier), most)
    wide = [scored(q, k * TOK, TOK) for k in whole_shards]
    for half in range(2):
        low = half * QROWS
        rows = slice(low, low + QROWS)
        near = scored(q[rows], last + low, QROWS)
        blocks = [(k * TOK, s[rows]) for k, s in zip(whole_shards, wide)]
        if earlier == most:
            far = scored(q[rows], low, QROWS)
            blocks.append((low, jnp.where(causal, masked_score, far)))
        blocks.append((last + low, jnp.where(causal, near, masked_score)))
        if half == 0 and earlier == most:
            blocks.append((QROWS, scored(q[rows], QROWS, QROWS)))
        if half == 1:
            blocks.append((last, scored(q[rows], last, QROWS)))
        tiles = [s[:, k : k + 128] for _, s in blocks for k in range(0, s.shape[1], 128)]
        peak = jnp.max(functools.reduce(jnp.maximum, tiles), axis=1, keepdims=True)
        weights = [jnp.exp(s - peak) for _, s in blocks]
        tiles = [p[:, k : k + 128] for p in weights for k in range(0, p.shape[1], 128)]
        norm = jnp.sum(functools.reduce(jnp.add, tiles), axis=1, keepdims=True)
        total = jnp.zeros((QROWS, HD), F32)
        for p, (begin, _) in zip(weights, blocks):
            total = total + jnp.dot(
                p.astype(BF16),
                kv[begin : begin + p.shape[1], HD:],
                preferred_element_type=F32,
            )
        out[rows, :] = (total / norm).astype(BF16)


def attend_kernel(info, q_ref, *refs):
    own, two, other, others = [refs[k * PARTS : (k + 1) * PARTS] for k in range(4)]
    out, kv = refs[-2:]
    core, position, place = (info[0], info[1], info[2])

    sources = (
        ((own, 0), (two, 1), (two, 0), (others, 0), (others, 1)),
        ((own, 0), (other, 0), (others, 1), (others, 0), (two, 0)),
    )
    for which in range(2):

        @pl.when((pl.program_id(0) == 0) & (core == which))
        def _():
            for k in range(PARTS):
                row = lax.rem(place + PARTS - k, PARTS) * QUARTER
                for behind, (pieces, slot) in enumerate(sources[which]):
                    there = (SHARDS - 1 - behind) * TOK + row
                    kv[pl.ds(pl.multiple_of(there, QUARTER), QUARTER), :] = pieces[k][
                        slot * QUARTER : (slot + 1) * QUARTER, :
                    ]

    for earlier in range(SHARDS):

        @pl.when(jnp.minimum(position, SHARDS - 1) == earlier)
        def _():
            attend_head(q_ref, kv, out, earlier)


def attend(head, count, info, queries, pieces, filled):
    block = pl.BlockSpec((TOK, HD), lambda h: (0, h + head))
    kept = pl.BlockSpec(memory_space=pl.ANY)
    inputs = (info, queries, *pieces)
    return pl.pallas_call(
        attend_kernel,
        name="attend",
        grid=(count,),
        out_shape=jax.ShapeDtypeStruct(queries.shape, BF16),
        in_specs=[SMEM, block] + [whole(piece.shape) for piece in pieces] + [kept] * len(filled),
        out_specs=block,
        scratch_shapes=[pltpu.VMEM((SHARDS * TOK, 2 * HD), BF16)],
        input_output_aliases={len(inputs) + k: k for k in range(len(filled))},
        compiler_params=pltpu.CompilerParams(vmem_limit_bytes=32 << 20),
        cost_estimate=pl.CostEstimate(
            flops=count << 30, bytes_accessed=4 << 20, transcendentals=count << 20
        ),
    )(*inputs, *filled)


def shards(
    branch_in,
    branch_gate,
    conv_taps,
    conv_shift,
    inflow_weight,
    inflow_bias,
    decay_weight,
    decay_bias,
    decay_param,
    stream,
    norm_gain,
    memory_weight,
    queries,
):
    position = lax.axis_index(SEQ)
    core = lax.axis_index(CORE)
    turn = lax.axis_index("mp")
    place = turn.reshape(1)
    info = jnp.stack([core, position, turn]).astype(jnp.int32)
    line = lambda v: v.reshape(1, -1)

    edge = shifted(branch_in[TOK - (CONV - 1) :], 1)
    parts = project(place, stream, line(norm_gain), memory_weight)
    edge, *parts = lax.optimization_barrier((edge, *parts))
    arrived = [turned(parts[k], k) for k in range(1, PARTS)]
    rest = (
        branch_gate, conv_taps, line(conv_shift), inflow_weight, line(inflow_bias),
        decay_weight, line(decay_bias), line(decay_param),
    )
    groups = branch_in.shape[1] // BLK
    u, w, couple = recur(0, groups, branch_in, edge, *rest, ())
    own_part, couple = lax.optimization_barrier((parts[0], couple))
    mine = normed([own_part] + arrived, couple)
    beside = swapped(mine)
    pair = jnp.concatenate([mine, beside])
    own = [turned(mine, k) for k in range(1, PARTS)]
    arrived, *own = lax.optimization_barrier((forked(pair, 1, 2), *own))
    duo, before, inclusive, got = window(info, pair, arrived, branch_in.shape[1])
    two = [turned(duo, k) for k in range(1, PARTS)]
    before, inclusive = merged(info, before, inclusive, got, swapped(got))
    far = forked(inclusive, 3, 6)
    far, two, own, duo = lax.optimization_barrier((far, two, own, duo))
    other = [swapped(piece) for piece in own]
    before, inclusive = merged(info, before, inclusive, far, swapped(far))
    two = [duo] + two
    others = [swapped(piece) for piece in two]
    far = [shifted(inclusive, 18 * k) for k in (1, 2, 3)]
    heads = queries.shape[1] // HD
    pieces = (mine, *own, *two, beside, *other, *others)
    attended = attend(0, heads, info, queries, pieces, ())
    *far, attended = lax.optimization_barrier((*far, attended))
    factor, state = (before[0:1], before[1:2])
    for couple in far:
        factor, state = (couple[0:1] * factor, factor * couple[1:2] + state)
    recurrent_out = (u + w * state).astype(BF16)
    return (recurrent_out, attended)


def solution(mesh):
    finer = Mesh(mesh.devices.reshape(8, 4, 2, mesh.shape["mp"]), (*SEQ, "mp"))
    in_specs = (
        P(SEQ, "mp"),
        P(SEQ, "mp"),
        P(None, "mp"),
        P("mp"),
        P("mp", None, None),
        P("mp"),
        P("mp", None, None),
        P("mp"),
        P("mp"),
        P(SEQ, "mp"),
        P("mp"),
        P("mp", None),
        P(SEQ, "mp"),
    )
    out_specs = (P(SEQ, "mp"), P(SEQ, "mp"))
    return jax.shard_map(
        shards, mesh=finer, in_specs=in_specs, out_specs=out_specs, check_vma=False
    )
```

```python
import functools

import jax
import jax.numpy as jnp
from jax import lax
from jax.experimental import pallas as pl
from jax.experimental.pallas import tpu as pltpu
from jax.sharding import Mesh
from jax.sharding import PartitionSpec as P

D = 4096
HD = 256
CONV = 4
WINDOW = 2048
BLK = 256
SEQ = ("seq_0", "seq_1", "seq_2")
CORE = "seq_2"
TOK = 512
QUARTER = 128
PARTS = 4
SEGMENTS = 8
STEPS = TOK // SEGMENTS
PITCH = STEPS + 1
QROWS = 256
LANES = 128
EXTRA = 16
ROOM = 60 << 20
SHARDS = 5

decay_power = 8.0
norm_epsilon = 1e-06
masked_score = -1e30
F32 = jnp.float32
BF16 = jnp.bfloat16
SMEM = pl.BlockSpec(memory_space=pltpu.SMEM)


def whole(shape):
    return pl.BlockSpec(shape, lambda *_: (0,) * len(shape))


def shifted(value, steps):
    count = lax.axis_size(SEQ)
    return lax.ppermute(value, SEQ, [(k, k + steps) for k in range(count - steps)])


def forked(value, near, distant):
    chips = lax.axis_size(SEQ) // 2
    pairs = [(2 * c, 2 * (c + near)) for c in range(chips - near)]
    pairs += [(2 * c + 1, 2 * (c + distant) + 1) for c in range(chips - distant)]
    return lax.ppermute(value, SEQ, pairs)


def turned(value, steps):
    return lax.ppermute(value, "mp", [(k, (k + steps) % PARTS) for k in range(PARTS)])


def swapped(value):
    return lax.ppermute(value, CORE, [(0, 1), (1, 0)])


def project_kernel(place, stream, gain, weight, *parts):
    row = lax.broadcasted_iota(jnp.int32, (EXTRA, QUARTER), 0)
    for k, part in enumerate(parts):
        start = pl.multiple_of(lax.rem(place[0] + k, PARTS) * QUARTER, QUARTER)
        x = stream[pl.ds(start, QUARTER), :].astype(F32)
        squares = jnp.sum(x * x, axis=1, keepdims=True)
        scaled = (x * gain[...]).astype(BF16)
        product = jnp.dot(scaled, weight[...], preferred_element_type=F32)
        part[0:QUARTER, :] = product.astype(part.dtype)
        part[QUARTER:, :] = jnp.zeros((EXTRA, 2 * HD), part.dtype)
        line = jnp.broadcast_to(squares, (QUARTER, QUARTER)).T[0:EXTRA]
        high = line.astype(BF16).astype(F32)
        line = jnp.where(row == 0, high, jnp.where(row == 1, line - high, 0.0))
        part[QUARTER:, 0:QUARTER] = line.astype(part.dtype)


def project(place, stream, gain, weight):
    shape = (QUARTER + EXTRA, 2 * HD)
    return pl.pallas_call(
        project_kernel,
        name="project",
        out_shape=[jax.ShapeDtypeStruct(shape, F32 if k == 0 else BF16) for k in range(PARTS)],
        in_specs=[SMEM, whole(stream.shape), whole(gain.shape), whole(weight.shape)],
        out_specs=[whole(shape)] * PARTS,
        compiler_params=pltpu.CompilerParams(vmem_limit_bytes=ROOM),
        cost_estimate=pl.CostEstimate(flops=1 << 29, bytes_accessed=3 << 20, transcendentals=0),
    )(place, stream, gain, weight)


def split(value):
    high = value.astype(BF16).astype(F32)
    rest = value - high
    middle = rest.astype(BF16).astype(F32)
    return (high, middle, rest - middle)


def norm_kernel(a, b, c, d, couple, out):
    total = (a[...] + b[...].astype(F32)) + (c[...].astype(F32) + d[...].astype(F32))
    line = total[QUARTER : QUARTER + 1, 0:QUARTER] + total[QUARTER + 1 : QUARTER + 2, 0:QUARTER]
    column = jnp.broadcast_to(line, (QUARTER, QUARTER)).T[:, 0:1]
    root = jnp.sqrt(column / D + norm_epsilon)
    out[0:QUARTER, :] = (total[0:QUARTER] / root).astype(BF16)
    width = 2 * HD
    lines = [
        part[:, k : k + width]
        for value in (couple[0:1, :], couple[1:2, :])
        for part in split(value)
        for k in range(0, value.shape[1], width)
    ]
    lines += [jnp.zeros((1, width), F32)] * (EXTRA - len(lines))
    out[QUARTER:, :] = jnp.concatenate(lines).astype(BF16)


def normed(parts, couple):
    shape = parts[0].shape
    return pl.pallas_call(
        norm_kernel,
        name="normed",
        out_shape=jax.ShapeDtypeStruct(shape, BF16),
        in_specs=[whole(shape)] * PARTS + [whole(couple.shape)],
        out_specs=whole(shape),
        compiler_params=pltpu.CompilerParams(vmem_limit_bytes=8 << 20),
        cost_estimate=pl.CostEstimate(flops=1 << 20, bytes_accessed=5 << 17, transcendentals=0),
    )(*parts, couple)


def received(lines, channels):
    values = []
    width = 2 * HD
    per = channels // width
    for value in range(2):
        halves = []
        for k in range(per):
            at = [value * 3 * per + part * per + k for part in range(3)]
            high, middle, low = [lines[row : row + 1] for row in at]
            halves.append(high + (middle + low))
        values.append(jnp.concatenate(halves, axis=1))
    return values


def applied(earlier, later):
    return (earlier[0] * later[0], later[0] * earlier[1] + later[1])


def chosen(flag, first, second):
    return [jnp.where(flag, x, y) for x, y in zip(first, second)]


def window_kernel(info, pair, arrived, duo, before, inclusive, got):
    channels = before.shape[1]
    first = info[0] == 0
    each = QUARTER + EXTRA
    duo[0:QUARTER, :] = arrived[0:QUARTER, :]
    duo[QUARTER:, :] = arrived[each : each + QUARTER, :]
    for ref, out in ((pair, inclusive), (arrived, got)):
        mine = received(ref[QUARTER:each, :].astype(F32), channels)
        theirs = received(ref[each + QUARTER :, :].astype(F32), channels)
        chip = applied(chosen(first, mine, theirs), chosen(first, theirs, mine))
        out[0:1, :], out[1:2, :] = chip
        if ref is pair:
            none = (jnp.ones_like(theirs[0]), jnp.zeros_like(theirs[1]))
            before[0:1, :], before[1:2, :] = chosen(first, none, theirs)


def window(info, pair, arrived, channels):
    shape = (2 * QUARTER, 2 * HD)
    couple = (2, channels)
    return pl.pallas_call(
        window_kernel,
        name="window",
        out_shape=[jax.ShapeDtypeStruct(shape, BF16)] + [jax.ShapeDtypeStruct(couple, F32)] * 3,
        in_specs=[SMEM] + [whole(pair.shape)] * 2,
        out_specs=[whole(shape)] + [whole(couple)] * 3,
        compiler_params=pltpu.CompilerParams(vmem_limit_bytes=8 << 20),
        cost_estimate=pl.CostEstimate(flops=1 << 14, bytes_accessed=3 << 18, transcendentals=0),
    )(info, pair, arrived)


def merge_kernel(info, before, inclusive, mine, theirs, before_out, inclusive_out):
    first = info[0] == 0
    passed = (before[0:1, :], before[1:2, :])
    covered = (inclusive[0:1, :], inclusive[1:2, :])
    for at in range(0, mine.shape[0], 2):
        ours = (mine[at : at + 1, :], mine[at + 1 : at + 2, :])
        other = (theirs[at : at + 1, :], theirs[at + 1 : at + 2, :])
        for earlier in (chosen(first, ours, other), chosen(first, other, ours)):
            passed = applied(earlier, passed)
            covered = applied(earlier, covered)
    before_out[0:1, :], before_out[1:2, :] = passed
    inclusive_out[0:1, :], inclusive_out[1:2, :] = covered


def merged(info, before, inclusive, mine, theirs):
    couple = whole(before.shape)
    return pl.pallas_call(
        merge_kernel,
        name="merged",
        out_shape=[jax.ShapeDtypeStruct(before.shape, F32)] * 2,
        in_specs=[SMEM, couple, couple, whole(mine.shape), whole(mine.shape)],
        out_specs=[couple, couple],
        compiler_params=pltpu.CompilerParams(vmem_limit_bytes=4 << 20),
        cost_estimate=pl.CostEstimate(flops=1 << 14, bytes_accessed=1 << 16, transcendentals=0),
    )(info, before, inclusive, mine, theirs)


def negative_expm1(y, grown):
    series = jnp.full_like(y, 1.0)
    for k in (8, 7, 6, 5, 4, 3, 2):
        series = 1.0 + series * (y * (1.0 / k))
    return jnp.where(y > -0.5, -y * series, 1.0 - grown)


def recur_kernel(
    branch, edge, gate, taps, shift, in_w, in_b, de_w, de_b, param, *rest
):
    u_out, w_out, end_out, extended, factors, pushes = rest[-6:]
    extended[8 : 8 + TOK, :] = branch[...].astype(F32)
    extended[8 - (CONV - 1) : 8, :] = edge[...].astype(F32)
    totals = shift[...] + taps[0:1, :] * extended[8 : 8 + TOK, :]
    for k in range(1, CONV):
        totals = totals + taps[k : k + 1, :] * extended[8 - k : 8 - k + TOK, :]
    mixed = totals.astype(BF16)
    inflow = jax.nn.sigmoid(
        jnp.dot(mixed, in_w[0], preferred_element_type=F32) + in_b[...]
    )
    recurrence = jax.nn.sigmoid(
        jnp.dot(mixed, de_w[0], preferred_element_type=F32) + de_b[...]
    )
    v = -param[...]
    soft = jnp.maximum(v, 0.0) + jnp.log1p(jnp.exp(-jnp.abs(v)))
    log_decay = recurrence * (-decay_power * soft)
    factor = jnp.exp(log_decay)
    push = (
        jnp.sqrt(negative_expm1(2.0 * log_decay, factor * factor))
        * inflow
        * mixed.astype(F32)
    )
    for lane in range(BLK // LANES):
        there = slice(lane * LANES, (lane + 1) * LANES)
        for r in range(SEGMENTS):
            rows = slice(r * STEPS, (r + 1) * STEPS)
            kept = slice(r * PITCH, r * PITCH + STEPS)
            factors[lane, kept, :] = factor[rows, there]
            pushes[lane, kept, :] = push[rows, there]

    lanes = range(BLK // LANES)
    product = [jnp.ones((SEGMENTS, LANES), F32) for _ in lanes]
    state = [jnp.zeros((SEGMENTS, LANES), F32) for _ in lanes]
    for t in range(STEPS):
        rows = pl.ds(t, SEGMENTS, stride=PITCH)
        for lane in lanes:
            f = factors[lane, rows, :]
            state[lane] = f * state[lane] + pushes[lane, rows, :]
            product[lane] = product[lane] * f
            pushes[lane, rows, :] = state[lane]
            factors[lane, rows, :] = product[lane]
    for lane in lanes:
        there = slice(lane * LANES, (lane + 1) * LANES)
        before_f = jnp.ones((1, LANES), F32)
        before_s = jnp.zeros((1, LANES), F32)
        for r in range(SEGMENTS):
            rows = slice(r * STEPS, (r + 1) * STEPS)
            g = gate[rows, there].astype(F32)
            g = 0.5 * g * (1.0 + jnp.tanh(0.7978845608028654 * (g + 0.044715 * (g * g * g))))
            kept = slice(r * PITCH, r * PITCH + STEPS)
            local_f = factors[lane, kept, :]
            u_out[rows, there] = (pushes[lane, kept, :] + local_f * before_s) * g
            w_out[rows, there] = (local_f * before_f) * g
            before_s = product[lane][r : r + 1] * before_s + state[lane][r : r + 1]
            before_f = product[lane][r : r + 1] * before_f
        end_out[0:1, there] = before_f
        end_out[1:2, there] = before_s


def recur(group, count, branch, edge, gate, taps, shift, in_w, in_b, de_w, de_b, param, filled):
    channels = branch.shape[1]
    lane = lambda rows: pl.BlockSpec((rows, BLK), lambda n: (0, n + group))
    square = pl.BlockSpec((1, BLK, BLK), lambda n: (n + group, 0, 0))
    kept = pl.BlockSpec(memory_space=pl.ANY)
    inputs = (branch, edge, gate, taps, shift, in_w, in_b, de_w, de_b, param)
    return pl.pallas_call(
        recur_kernel,
        name="recur",
        grid=(count,),
        out_shape=[
            jax.ShapeDtypeStruct((TOK, channels), F32),
            jax.ShapeDtypeStruct((TOK, channels), F32),
            jax.ShapeDtypeStruct((2, channels), F32),
        ],
        in_specs=[
            lane(TOK), lane(CONV - 1), lane(TOK), lane(CONV), lane(1),
            square, lane(1), square, lane(1), lane(1),
        ] + [kept] * len(filled),
        out_specs=[lane(TOK), lane(TOK), lane(2)],
        scratch_shapes=[
            pltpu.VMEM((TOK + 8, BLK), F32),
            pltpu.VMEM((BLK // LANES, SEGMENTS * PITCH, LANES), F32),
            pltpu.VMEM((BLK // LANES, SEGMENTS * PITCH, LANES), F32),
        ],
        input_output_aliases={len(inputs) + k: k for k in range(len(filled))},
        compiler_params=pltpu.CompilerParams(vmem_limit_bytes=ROOM),
        cost_estimate=pl.CostEstimate(
            flops=count << 28, bytes_accessed=count << 21, transcendentals=count << 20
        ),
    )(*inputs, *filled)


def attend_head(q_ref, kv, out, earlier):
    def scored(q, begin, size):
        return lax.dot_general(
            q,
            kv[begin : begin + size, 0:HD],
            (((1,), (1,)), ((), ())),
            preferred_element_type=F32,
        )

    rows = lax.broadcasted_iota(jnp.int32, (QROWS, QROWS), 0)
    columns = lax.broadcasted_iota(jnp.int32, (QROWS, QROWS), 1)
    causal = rows >= columns
    last = (SHARDS - 1) * TOK
    q = q_ref[...] * jnp.asarray(HD**-0.5, BF16)
    most = SHARDS - 1
    whole_shards = range(max(1, most - earlier), most)
    wide = [scored(q, k * TOK, TOK) for k in whole_shards]
    for half in range(2):
        low = half * QROWS
        rows = slice(low, low + QROWS)
        near = scored(q[rows], last + low, QROWS)
        blocks = [(k * TOK, s[rows]) for k, s in zip(whole_shards, wide)]
        if earlier == most:
            far = scored(q[rows], low, QROWS)
            blocks.append((low, jnp.where(causal, masked_score, far)))
        blocks.append((last + low, jnp.where(causal, near, masked_score)))
        if half == 0 and earlier == most:
            blocks.append((QROWS, scored(q[rows], QROWS, QROWS)))
        if half == 1:
            blocks.append((last, scored(q[rows], last, QROWS)))
        tiles = [s[:, k : k + 128] for _, s in blocks for k in range(0, s.shape[1], 128)]
        peak = jnp.max(functools.reduce(jnp.maximum, tiles), axis=1, keepdims=True)
        weights = [jnp.exp(s - peak) for _, s in blocks]
        tiles = [p[:, k : k + 128] for p in weights for k in range(0, p.shape[1], 128)]
        norm = jnp.sum(functools.reduce(jnp.add, tiles), axis=1, keepdims=True)
        total = jnp.zeros((QROWS, HD), F32)
        for p, (begin, _) in zip(weights, blocks):
            total = total + jnp.dot(
                p.astype(BF16),
                kv[begin : begin + p.shape[1], HD:],
                preferred_element_type=F32,
            )
        out[rows, :] = (total / norm).astype(BF16)


def attend_kernel(info, q_ref, *refs):
    own, two, other, others = [refs[k * PARTS : (k + 1) * PARTS] for k in range(4)]
    out, kv = refs[-2:]
    core, position, place = (info[0], info[1], info[2])

    sources = (
        ((own, 0), (two, 1), (two, 0), (others, 0), (others, 1)),
        ((own, 0), (other, 0), (others, 1), (others, 0), (two, 0)),
    )
    for which in range(2):

        @pl.when((pl.program_id(0) == 0) & (core == which))
        def _():
            for k in range(PARTS):
                row = lax.rem(place + PARTS - k, PARTS) * QUARTER
                for behind, (pieces, slot) in enumerate(sources[which]):
                    there = (SHARDS - 1 - behind) * TOK + row
                    kv[pl.ds(pl.multiple_of(there, QUARTER), QUARTER), :] = pieces[k][
                        slot * QUARTER : (slot + 1) * QUARTER, :
                    ]

    for earlier in range(SHARDS):

        @pl.when(jnp.minimum(position, SHARDS - 1) == earlier)
        def _():
            attend_head(q_ref, kv, out, earlier)


def attend(head, count, info, queries, pieces, filled):
    block = pl.BlockSpec((TOK, HD), lambda h: (0, h + head))
    kept = pl.BlockSpec(memory_space=pl.ANY)
    inputs = (info, queries, *pieces)
    return pl.pallas_call(
        attend_kernel,
        name="attend",
        grid=(count,),
        out_shape=jax.ShapeDtypeStruct(queries.shape, BF16),
        in_specs=[SMEM, block] + [whole(piece.shape) for piece in pieces] + [kept] * len(filled),
        out_specs=block,
        scratch_shapes=[pltpu.VMEM((SHARDS * TOK, 2 * HD), BF16)],
        input_output_aliases={len(inputs) + k: k for k in range(len(filled))},
        compiler_params=pltpu.CompilerParams(vmem_limit_bytes=32 << 20),
        cost_estimate=pl.CostEstimate(
            flops=count << 30, bytes_accessed=4 << 20, transcendentals=count << 20
        ),
    )(*inputs, *filled)


def shards(
    branch_in,
    branch_gate,
    conv_taps,
    conv_shift,
    inflow_weight,
    inflow_bias,
    decay_weight,
    decay_bias,
    decay_param,
    stream,
    norm_gain,
    memory_weight,
    queries,
):
    position = lax.axis_index(SEQ)
    core = lax.axis_index(CORE)
    turn = lax.axis_index("mp")
    place = turn.reshape(1)
    info = jnp.stack([core, position, turn]).astype(jnp.int32)
    line = lambda v: v.reshape(1, -1)

    edge = shifted(branch_in[TOK - (CONV - 1) :], 1)
    parts = project(place, stream, line(norm_gain), memory_weight)
    edge, *parts = lax.optimization_barrier((edge, *parts))
    arrived = [turned(parts[k], k) for k in range(1, PARTS)]
    rest = (
        branch_gate, conv_taps, line(conv_shift), inflow_weight, line(inflow_bias),
        decay_weight, line(decay_bias), line(decay_param),
    )
    groups = branch_in.shape[1] // BLK
    u, w, couple = recur(0, groups, branch_in, edge, *rest, ())
    own_part, couple = lax.optimization_barrier((parts[0], couple))
    mine = normed([own_part] + arrived, couple)
    beside = swapped(mine)
    pair = jnp.concatenate([mine, beside])
    own = [turned(mine, k) for k in range(1, PARTS)]
    arrived, *own = lax.optimization_barrier((forked(pair, 1, 2), *own))
    duo, before, inclusive, got = window(info, pair, arrived, branch_in.shape[1])
    two = [turned(duo, k) for k in range(1, PARTS)]
    before, inclusive = merged(info, before, inclusive, got, swapped(got))
    far = [forked(inclusive, 3, 6), forked(inclusive, 9, 12)]
    far, two, own, duo = lax.optimization_barrier((far, two, own, duo))
    other = [swapped(piece) for piece in own]
    far = jnp.concatenate(far)
    before, inclusive = merged(info, before, inclusive, far, swapped(far))
    two = [duo] + two
    others = [swapped(piece) for piece in two]
    far = [shifted(inclusive, 30), shifted(inclusive, 60)]
    heads = queries.shape[1] // HD
    pieces = (mine, *own, *two, beside, *other, *others)
    attended = attend(0, heads, info, queries, pieces, ())
    *far, attended = lax.optimization_barrier((*far, attended))
    state = far[0][0:1] * far[1][1:2] + far[0][1:2]
    state = before[0:1] * state + before[1:2]
    recurrent_out = (u + w * state).astype(BF16)
    return (recurrent_out, attended)


def solution(mesh):
    finer = Mesh(mesh.devices.reshape(8, 4, 2, mesh.shape["mp"]), (*SEQ, "mp"))
    in_specs = (
        P(SEQ, "mp"),
        P(SEQ, "mp"),
        P(None, "mp"),
        P("mp"),
        P("mp", None, None),
        P("mp"),
        P("mp", None, None),
        P("mp"),
        P("mp"),
        P(SEQ, "mp"),
        P("mp"),
        P("mp", None),
        P(SEQ, "mp"),
    )
    out_specs = (P(SEQ, "mp"), P(SEQ, "mp"))
    return jax.shard_map(
        shards, mesh=finer, in_specs=in_specs, out_specs=out_specs, check_vma=False
    )
```
